512 devices in a mesh: ex: 128 (over y, x, z_lo), tok: 4 (over z_hi, core).
Axes of the slice: x: 4, y: 4, z: 16 (z_hi: 2, z_lo: 8; z = z_hi * 8 + z_lo), core: 2. Of those that a mesh axis runs over, the one named last changes fastest.
Arguments:
- proj_rows: bfloat16 [1048576, 128], P(('ex', 'tok')), may hold values from -6 to 6
- query_features: bfloat16 [8192, 4096], P('ex'), may hold values from -0.09375 to 0.09375
- doc_lengths: int32 [128, 32], P('ex'), may hold values from 1 to 4096, 8192 in all within a row
- owner_map: int32 [128, 32], P('ex'), may hold values from 0 to 31, each once within a row
Outputs:
- scores: float32 [8192, 4096], P('ex', 'tok')
The draws below stay inside these ranges and needn't reach their ends.
Inputs may be any that keep to these rules, and one draw needn't show every extreme that they name: `owner_map`: each row lists the slots 0 to 31 once each. `doc_lengths`: each row sums to 8192; its largest entry is exactly 4096.
All inputs are finite; a program needn't handle non-finite values.
Results may differ from the reference program's by a relative error of at most 0.0029.
Values may be sent and summed in bfloat16 or wider, within the bound.
A program may use at most 64 MiB of HBM per device.

```python
import math
import jax
import jax.numpy as jnp
import numpy as np
from jax import lax

P_SIZE = 64
FEAT = 4096
DOC_DEV = 8
TOK_GROUP = 8192
DOC_GROUP = 32
LEN_MOST = 4096
TOKENS = 1048576
DOCS = 4096
QUERIES = 8192
N_EX = 128
N_TOK = 4


def block_scale(key, shape, cuts, smallest, high):
    def one(axis_at, blocks):
        heights = jax.random.uniform(jax.random.fold_in(jax.random.fold_in(key, 6), axis_at), (blocks,), jnp.float32, smallest / len(cuts), high / len(cuts))
        return jnp.repeat(jnp.exp(heights), shape[axis_at] // blocks).reshape((-1,) + (1,) * (len(shape) - axis_at - 1))

    level = one(*cuts[0])
    for cut in cuts[1:]:
        level = level * one(*cut)
    return level


def profile(count, total, bound, lean):
    loads = [(1 << 20) // math.isqrt(grade ** lean) + 1 for grade in range(2, count + 1)]
    rest, holding = total - bound - (count - 1), [1] * (count - 1)
    while rest > 0:
        free = [i for i in range(count - 1) if holding[i] < bound]
        whole, budget = sum([loads[i] for i in free]), rest
        for i in free:
            extra = min(bound - holding[i], max(1, budget * loads[i] // whole), rest)
            holding[i] = holding[i] + extra
            rest = rest - extra
    return np.array([bound] + holding)


def ragged_sizes(rng, amount, total, bound, lean):
    if amount == 2:
        one = jax.random.randint(rng, (), max(1, total - bound), min(bound, total - 1) + 1)
        return jnp.stack([one, total - one])
    sizes = jnp.asarray(profile(amount, total, bound, lean), jnp.int32)
    twos = (amount - 1) // 2
    giver, receiver = sizes[1:1 + 2 * twos:2], sizes[2:2 + 2 * twos:2]
    room = jnp.minimum(giver - 1, bound - receiver)
    shifted = jax.random.randint(jax.random.fold_in(rng, 1), (twos,), 0, 1 << 20) % (room + 1)
    sizes = sizes.at[1:1 + 2 * twos:2].set(giver - shifted).at[2:2 + 2 * twos:2].set(receiver + shifted)
    return sizes[jax.random.permutation(jax.random.fold_in(rng, 2), amount)]


def centred(stream_key, dims, deviation, limit, split=(), kind=jnp.bfloat16):
    gain = block_scale(stream_key, dims, split, -0.22, 0.18) if split else 1.0
    result = jax.random.normal(stream_key, dims, jnp.float32) * deviation * gain
    return jnp.minimum(jnp.maximum(result, -limit), limit).astype(kind)


def setup_inputs(seed: int = 0) -> dict:
    keys = jax.random.split(jax.random.key(seed), 5)
    proj_rows = centred(keys[0], (TOKENS, 2 * P_SIZE), 1.0, 6.0, ((0, 512),))
    query_features = centred(keys[1], (QUERIES, FEAT), FEAT ** -0.5, 0.09375, ((0, 128),))
    doc_lengths = jax.vmap(lambda own: ragged_sizes(own, DOC_GROUP, TOK_GROUP, LEN_MOST, 2))(jax.random.split(keys[2], N_EX)).reshape((N_EX, DOC_GROUP)).astype(jnp.int32)
    owner_map = jax.vmap(lambda own: jax.random.permutation(own, DOC_GROUP))(jax.random.split(keys[3], N_EX)).reshape((N_EX, DOC_GROUP)).astype(jnp.int32)
    return dict(proj_rows=proj_rows, query_features=query_features, doc_lengths=doc_lengths, owner_map=owner_map)


def group_features(packed):
    group_rows, group_lengths, owner_slots = packed
    doc_ends = jnp.cumsum(group_lengths)
    positions = jnp.arange(TOK_GROUP, dtype=jnp.int32)
    doc_index = lax.optimization_barrier(jnp.sum((positions[:, None] >= doc_ends[None, :]).astype(jnp.int32), axis=1))
    onehot = (doc_index[:, None] == jnp.arange(DOC_GROUP, dtype=jnp.int32)[None, :]).astype(jnp.float32)
    input_rows = group_rows[:, :P_SIZE].astype(jnp.float32)
    grad_rows = group_rows[:, P_SIZE:].astype(jnp.float32)
    spread = (onehot[:, :, None] * grad_rows[:, None, :]).reshape(TOK_GROUP, DOC_GROUP * P_SIZE)
    kron_sum = jnp.dot(spread.T, input_rows, precision=lax.Precision.HIGHEST).reshape(DOC_GROUP, P_SIZE * P_SIZE)
    features = kron_sum / jnp.sqrt(group_lengths.astype(jnp.float32))[:, None]
    placed = jnp.zeros((DOC_GROUP, P_SIZE * P_SIZE), jnp.float32).at[owner_slots].set(features)
    return placed.astype(jnp.bfloat16)

def reference(proj_rows, query_features, doc_lengths, owner_map):
    grouped = proj_rows.reshape(N_EX, TOK_GROUP, 2 * P_SIZE)
    features = lax.map(group_features, (grouped, doc_lengths, owner_map))
    doc_features = features.reshape(N_EX, N_TOK, DOC_DEV, P_SIZE * P_SIZE).transpose(1, 0, 2, 3).reshape(DOCS, P_SIZE * P_SIZE)
    return jnp.dot(query_features, doc_features.T, preferred_element_type=jnp.float32)
```

```python
import jax
import jax.numpy as jnp
from jax import lax
from jax.experimental import pallas as pl
from jax.experimental.pallas import tpu as pltpu
from jax.sharding import PartitionSpec as P

MESH = pl.DeviceIdType.MESH
F32 = jnp.float32
BF16 = jnp.bfloat16


def kernel(
    rows_ref, lens_ref, owner_ref, q_hbm, out_ref,
    xx, gt, mask, part, sib_recv, dsend, drecv, dall, qa, qb, sc_a, sc_b, pk, pk_recv, fin, fin_recv,
    sib_s, sib_r, q1_s, q1_r, q2_s, q2_r, ql, pi_s, pi_r, sw_s, sw_r, qd_s, qd_r, s2_s, s2_r, o_s, o_r,
):
    ex, tok = lax.axis_index("ex"), lax.axis_index("tok")
    y, x, p = ex // 32, lax.rem(ex // 8, 4), lax.rem(ex, 8)
    h, c = tok // 2, lax.rem(tok, 2)
    b, k = p // 4, lax.rem(p, 4)

    def at(yy, xx_, pp, hh, cc):
        return {"ex": (yy * 4 + xx_) * 8 + pp, "tok": hh * 2 + cc}

    def plane(dy, dx):
        return at(lax.rem(y + dy, 4), lax.rem(x + dx, 4), p, h, c)

    far = lax.rem(p + 4, 8)
    sibling = at(y, x, p, h, 1 - c)
    near_far = at(y, x, far, h, c)
    other_far = at(y, x, far, 1 - h, c)

    def quad(d):
        return at(y, x, b * 4 + lax.rem(k + d, 4), h, c)

    offsets = [(dy, dx) for dy in range(4) for dx in range(4) if dy or dx]
    partners = [plane(*o) for o in offsets] + [quad(d) for d in (1, 2, 3)] + [sibling, near_far, other_far]

    barrier = pltpu.get_barrier_semaphore()
    for partner in partners:
        pl.semaphore_signal(barrier, inc=1, device_id=partner, device_id_type=MESH)

    lens = lens_ref[...].astype(F32)
    owner = owner_ref[...]
    lane = lax.broadcasted_iota(jnp.int32, (32, 32), 1)
    slot = lax.broadcasted_iota(jnp.int32, (32, 32), 0)
    match = jnp.broadcast_to(owner, (32, 32)) == slot
    lens_b = jnp.broadcast_to(lens, (32, 32))
    order = jnp.sum(jnp.where(match, lane.astype(F32), 0.0), axis=1, keepdims=True)
    size = jnp.sum(jnp.where(match, lens_b, 0.0), axis=1, keepdims=True)
    begin = jnp.sum(jnp.where(lane.astype(F32) < order, lens_b, 0.0), axis=1, keepdims=True)
    end = begin + size
    scale = 1.0 / jnp.sqrt(size)
    pos = (lax.broadcasted_iota(jnp.int32, (32, 2048), 1) + tok * 2048).astype(F32)
    mask[...] = jnp.where((pos >= begin) & (pos < end), 1.0, 0.0)

    pick_r = lax.broadcasted_iota(jnp.int32, (64, 128), 0)
    pick_c = lax.broadcasted_iota(jnp.int32, (64, 128), 1)
    pick_g = (pick_c == pick_r + 64).astype(BF16)
    gt[...] = lax.dot_general(pick_g, rows_ref[...], (((1,), (1,)), ((), ())), preferred_element_type=F32)
    twice_r = lax.broadcasted_iota(jnp.int32, (128, 128), 0)
    twice_c = lax.broadcasted_iota(jnp.int32, (128, 128), 1)
    twice = ((twice_r == twice_c) | (twice_r + 64 == twice_c)).astype(F32)
    twice = jnp.where(twice_r < 64, twice, 0.0).astype(BF16)
    xx[...] = jnp.dot(rows_ref[...], twice, preferred_element_type=F32).astype(BF16)

    low = lax.broadcasted_iota(jnp.int32, (32, 128), 1) < 64

    def kron_half(half, dest):
        def step(n, carry):
            blocks = []
            for i in range(16):
                g_row = gt[pl.ds(half * 32 + n * 16 + i, 1), :]
                blocks.append((mask[...] * g_row).astype(BF16))
            spread = jnp.concatenate(blocks, axis=0)
            res = jnp.dot(spread, xx[...], preferred_element_type=F32)
            for i in range(8):
                even = res[64 * i:64 * i + 32]
                odd = res[64 * i + 32:64 * i + 64]
                dest[:, pl.ds(pl.multiple_of((n * 8 + i) * 128, 128), 128)] = jnp.where(low, even, odd)
            return carry

        lax.fori_loop(0, 2, step, 0)

    kron_half(1 - c, part.at[0])
    pl.semaphore_wait(barrier, len(partners))

    def send(src, dst, ss, rs, to):
        cp = pltpu.make_async_remote_copy(
            src_ref=src, dst_ref=dst, send_sem=ss, recv_sem=rs, device_id=to, device_id_type=MESH
        )
        cp.start()
        return cp

    sib = send(part.at[0], sib_recv, sib_s, sib_r, sibling)

    cols_a = pl.ds(pl.multiple_of(c * 2048, 1024), 1024)
    cols_b = pl.ds(pl.multiple_of(c * 2048 + 1024, 1024), 1024)
    q1 = []
    for n, d in enumerate((1, 2, 3)):
        q1.append(send(q_hbm.at[:, cols_a], qa.at[y, x], q1_s.at[n], q1_r.at[n], plane(0, d)))
        q1.append(send(q_hbm.at[:, cols_b], qb.at[x, y], q1_s.at[n + 3], q1_r.at[n + 3], plane(d, 0)))
    own_a = pltpu.make_async_copy(q_hbm.at[:, cols_a], qa.at[y, x], ql.at[0])
    own_b = pltpu.make_async_copy(q_hbm.at[:, cols_b], qb.at[x, y], ql.at[1])
    own_a.start()
    own_b.start()

    kron_half(c, part.at[1])
    sib.wait_recv()
    feats = ((part[1] + sib_recv[...]) * scale).astype(BF16)
    dsend[0] = feats[:16]
    dsend[1] = feats[16:]
    pi = [
        send(dsend.at[h], drecv.at[0], pi_s.at[0], pi_r.at[0], near_far),
        send(dsend.at[1 - h], drecv.at[1], pi_s.at[1], pi_r.at[1], other_far),
    ]

    own_a.wait()
    own_b.wait()
    for cp in q1:
        cp.wait()
    q2 = []
    for n, d in enumerate((1, 2, 3)):
        q2.append(send(qa.at[y], qa.at[y], q2_s.at[n], q2_r.at[n], plane(d, 0)))
        q2.append(send(qb.at[x], qb.at[x], q2_s.at[n + 3], q2_r.at[n + 3], plane(0, d)))

    for cp in pi:
        cp.wait_recv()
    dall[k, 1 - b] = (drecv[0].astype(F32) + drecv[1].astype(F32)).astype(BF16)
    sw = send(dall.at[k, 1 - b], dall.at[k, 1 - b], sw_s, sw_r, near_far)
    qd = [send(dall.at[k, 1 - b], dall.at[k, 1 - b], qd_s.at[n], qd_r.at[n], quad(n + 1)) for n in range(3)]
    sw.wait_recv()
    qd += [send(dall.at[k, b], dall.at[k, b], qd_s.at[n + 3], qd_r.at[n + 3], quad(n + 1)) for n in range(3)]
    for cp in qd:
        cp.wait_recv()

    wide = [dall[g % 4, g // 4].astype(F32) for g in range(8)]
    docs = jnp.concatenate([w[:8] for w in wide] + [w[8:] for w in wide], axis=0).astype(BF16)
    for cp in q2:
        cp.wait_recv()
    nt = (((1,), (1,)), ((), ()))
    sc_a[...] = lax.dot_general(qa[...].reshape(1024, 1024), docs[:, :1024], nt, preferred_element_type=F32).reshape(4, 4, 64, 128)
    sc_b[...] = lax.dot_general(qb[...].reshape(1024, 1024), docs[:, 1024:], nt, preferred_element_type=F32).reshape(4, 4, 64, 128)

    for gy in range(4):
        for gx in range(4):
            s = sc_a[gy, gx] + sc_b[gx, gy]
            top, bottom = s[:32], s[32:]
            pk[0, gy, gx] = jnp.where(low, top, pltpu.roll(bottom, 64, 1))
            pk[1, gy, gx] = jnp.where(low, pltpu.roll(top, 64, 1), bottom)
    s2 = send(pk.at[1 - c], pk_recv, s2_s, s2_r, sibling)
    s2.wait_recv()
    fin[...] = pk[c] + pk_recv[...]
    os = []
    for n, (dy, dx) in enumerate(offsets):
        os.append(send(
            fin.at[lax.rem(y + dy, 4), lax.rem(x + dx, 4)], fin_recv.at[y, x], o_s.at[n], o_r.at[n], plane(dy, dx)
        ))
    fin_recv[y, x] = fin[y, x]
    for cp in os:
        cp.wait_recv()
    for n in range(8):
        first, second = fin_recv[n // 2, 2 * (n % 2)], fin_recv[n // 2, 2 * (n % 2) + 1]
        out_ref[:32, n * 128:(n + 1) * 128] = jnp.where(low, first, pltpu.roll(second, 64, 1))
        out_ref[32:, n * 128:(n + 1) * 128] = jnp.where(low, pltpu.roll(first, 64, 1), second)

    for cp in [sib, *pi, *q2, sw, *qd, s2, *os]:
        cp.wait_send()


def body(proj_rows, query_features, doc_lengths, owner_map):
    vmem = pl.BlockSpec(memory_space=pltpu.VMEM)
    dma = pltpu.SemaphoreType.DMA
    return pl.pallas_call(
        kernel,
        name="scores",
        out_shape=jax.ShapeDtypeStruct((64, 1024), F32),
        in_specs=[vmem, vmem, vmem, pl.BlockSpec(memory_space=pl.ANY)],
        out_specs=vmem,
        scratch_shapes=[
            pltpu.VMEM((2048, 128), BF16),
            pltpu.VMEM((64, 2048), F32),
            pltpu.VMEM((32, 2048), F32),
            pltpu.VMEM((2, 32, 2048), F32),
            pltpu.VMEM((32, 2048), F32),
            pltpu.VMEM((2, 16, 2048), BF16),
            pltpu.VMEM((2, 16, 2048), BF16),
            pltpu.VMEM((4, 2, 16, 2048), BF16),
            pltpu.VMEM((4, 4, 64, 1024), BF16),
            pltpu.VMEM((4, 4, 64, 1024), BF16),
            pltpu.VMEM((4, 4, 64, 128), F32),
            pltpu.VMEM((4, 4, 64, 128), F32),
            pltpu.VMEM((2, 4, 4, 32, 128), F32),
            pltpu.VMEM((4, 4, 32, 128), F32),
            pltpu.VMEM((4, 4, 32, 128), F32),
            pltpu.VMEM((4, 4, 32, 128), F32),
            dma, dma, dma((6,)), dma((6,)), dma((6,)), dma((6,)), dma((2,)),
            dma((2,)), dma((2,)), dma, dma, dma((6,)), dma((6,)), dma, dma, dma((15,)), dma((15,)),
        ],
        compiler_params=pltpu.CompilerParams(
            collective_id=0, has_side_effects=True, vmem_limit_bytes=48 << 20
        ),
    )(proj_rows, doc_lengths, owner_map, query_features)


def solution(mesh):
    placed = (P(("ex", "tok"), None), P("ex", None), P("ex", None), P("ex", None))
    return jax.shard_map(
        body, mesh=mesh, in_specs=placed, out_specs=P("ex", "tok"), check_vma=False
    )
```

```python
import jax
import jax.numpy as jnp
from jax import lax
from jax.experimental import pallas as pl
from jax.experimental.pallas import tpu as pltpu
from jax.sharding import PartitionSpec as P

MESH = pl.DeviceIdType.MESH
F32 = jnp.float32
BF16 = jnp.bfloat16


def kernel(
    rows_hbm, lens_hbm, owner_hbm, q_hbm, out_ref,
    rows_ref, lens_ref, owner_ref,
    xx, gt, mask, part, sib_recv, dsend, drecv, dall, qa, qb, sc_a, sc_b, pk, pk_recv, fin, fin_recv,
    in_l, ql, sib_s, sib_r, qs, qr, pi_s, pi_r, sw_s, sw_r, f_s, f_r, g_s, g_r, s2_s, s2_r, o_s, o_r,
):
    ex, tok = lax.axis_index("ex"), lax.axis_index("tok")
    y, x, p = ex // 32, lax.rem(ex // 8, 4), lax.rem(ex, 8)
    h, c = tok // 2, lax.rem(tok, 2)
    b, k = p // 4, lax.rem(p, 4)

    def at(yy, xx_, pp, hh, cc):
        return {"ex": (yy * 4 + xx_) * 8 + pp, "tok": hh * 2 + cc}

    def plane(dy, dx):
        return at(lax.rem(y + dy, 4), lax.rem(x + dx, 4), p, h, c)

    loads = [
        pltpu.make_async_copy(src, dst, in_l.at[n])
        for n, (src, dst) in enumerate(((lens_hbm, lens_ref), (owner_hbm, owner_ref), (rows_hbm, rows_ref)))
    ]
    for cp in loads:
        cp.start()

    far = lax.rem(p + 4, 8)
    sibling = at(y, x, p, h, 1 - c)
    near_far = at(y, x, far, h, c)
    other_far = at(y, x, far, 1 - h, c)

    flip3 = at(y, x, b * 4 + 3 - k, h, c)
    flip1 = at(y, x, p + 1 - 2 * lax.rem(p, 2), h, c)

    offsets = [(dy, dx) for dy in range(4) for dx in range(4) if dy or dx]
    partners = [plane(*o) for o in offsets] + [flip3, flip1, sibling, near_far, other_far]

    barrier = pltpu.get_barrier_semaphore()
    for partner in partners:
        pl.semaphore_signal(barrier, inc=1, device_id=partner, device_id_type=MESH)

    loads[0].wait()
    loads[1].wait()
    lens = lens_ref[...].astype(F32)
    owner = owner_ref[...]
    lane = lax.broadcasted_iota(jnp.int32, (32, 32), 1)
    slot = lax.broadcasted_iota(jnp.int32, (32, 32), 0)
    match = jnp.broadcast_to(owner, (32, 32)) == slot
    lens_b = jnp.broadcast_to(lens, (32, 32))
    order = jnp.sum(jnp.where(match, lane.astype(F32), 0.0), axis=1, keepdims=True)
    size = jnp.sum(jnp.where(match, lens_b, 0.0), axis=1, keepdims=True)
    begin = jnp.sum(jnp.where(lane.astype(F32) < order, lens_b, 0.0), axis=1, keepdims=True)
    end = begin + size
    scale = 1.0 / jnp.sqrt(size)
    pos = (lax.broadcasted_iota(jnp.int32, (32, 2048), 1) + tok * 2048).astype(F32)
    mask[...] = jnp.where((pos >= begin) & (pos < end), 1.0, 0.0)

    loads[2].wait()
    pick_r = lax.broadcasted_iota(jnp.int32, (64, 128), 0)
    pick_c = lax.broadcasted_iota(jnp.int32, (64, 128), 1)
    pick_g = (pick_c == pick_r + 64).astype(BF16)
    gt[...] = lax.dot_general(pick_g, rows_ref[...], (((1,), (1,)), ((), ())), preferred_element_type=F32)
    twice_r = lax.broadcasted_iota(jnp.int32, (128, 128), 0)
    twice_c = lax.broadcasted_iota(jnp.int32, (128, 128), 1)
    twice = ((twice_r == twice_c) | (twice_r + 64 == twice_c)).astype(F32)
    twice = jnp.where(twice_r < 64, twice, 0.0).astype(BF16)
    xx[...] = jnp.dot(rows_ref[...], twice, preferred_element_type=F32).astype(BF16)

    low = lax.broadcasted_iota(jnp.int32, (32, 128), 1) < 64

    def kron_half(half, dest):
        def step(n, carry):
            blocks = []
            for i in range(16):
                g_row = gt[pl.ds(half * 32 + n * 16 + i, 1), :]
                blocks.append((mask[...] * g_row).astype(BF16))
            spread = jnp.concatenate(blocks, axis=0)
            res = jnp.dot(spread, xx[...], preferred_element_type=F32)
            for i in range(8):
                even = res[64 * i:64 * i + 32]
                odd = res[64 * i + 32:64 * i + 64]
                dest[:, pl.ds(pl.multiple_of((n * 8 + i) * 128, 128), 128)] = jnp.where(low, even, odd)
            return carry

        lax.fori_loop(0, 2, step, 0)

    kron_half(1 - c, part.at[0])
    pl.semaphore_wait(barrier, len(partners))

    def send(src, dst, ss, rs, to):
        cp = pltpu.make_async_remote_copy(
            src_ref=src, dst_ref=dst, send_sem=ss, recv_sem=rs, device_id=to, device_id_type=MESH
        )
        cp.start()
        return cp

    sib = send(part.at[0], sib_recv, sib_s, sib_r, sibling)

    halves = ((qa, y, x, lambda d: plane(0, d), lambda d: plane(d, 0)), (qb, x, y, lambda d: plane(d, 0), lambda d: plane(0, d)))
    steps = (1, 3)

    started = []

    def q_send(n, src, dst, sem, to):
        cp = send(src, dst, qs.at[n, sem], qr.at[n, sem], to)
        started.append(cp)
        return cp

    parts = (pl.ds(0, 32), pl.ds(32, 32))
    first, rest = [], []
    for n, (buf, r, s, ring, cross) in enumerate(halves):
        cols = pl.ds(pl.multiple_of(c * 2048 + n * 1024, 1024), 1024)
        own = pltpu.make_async_copy(q_hbm.at[:, cols], buf.at[r, s], ql.at[n])
        own.start()
        rest.append(own)
        for i, d in enumerate(steps):
            first.append(q_send(n, q_hbm.at[:, cols], buf.at[r, s], i, ring(d)))
    cross_own = []
    for n, (buf, r, s, ring, cross) in enumerate(halves):
        cols = pl.ds(pl.multiple_of(c * 2048 + n * 1024, 1024), 1024)
        for i, d in enumerate(steps):
            cross_own.append(q_send(n, q_hbm.at[:, cols], buf.at[r, s], 2 + i, cross(d)))

    def hop_ring():
        out = []
        for n, (buf, r, s, ring, cross) in enumerate(halves):
            for i, d in enumerate(steps):
                blk = buf.at[r, lax.rem(s + 4 - d, 4), parts[i]]
                out.append(q_send(n, blk, blk, 4 + i, ring(d)))
        return out

    def hop_cross(e, base):
        out = []
        for n, (buf, r, s, ring, cross) in enumerate(halves):
            blk = buf.at[r, lax.rem(s + e, 4)]
            for i, d in enumerate(steps):
                out.append(q_send(n, blk, blk, base + i, cross(d)))
        return out

    def hop_cross_on(e, base):
        out = []
        for n, (buf, r, s, ring, cross) in enumerate(halves):
            for i, d in enumerate(steps):
                blk = buf.at[lax.rem(r + 4 - d, 4), lax.rem(s + e, 4), parts[i]]
                out.append(q_send(n, blk, blk, base + i, cross(d)))
        return out

    kron_half(c, part.at[1])
    sib.wait_recv()
    feats = ((part[1] + sib_recv[...]) * scale).astype(BF16)
    dsend[0] = feats[:16]
    dsend[1] = feats[16:]
    pi = [
        send(dsend.at[h], drecv.at[0], pi_s.at[0], pi_r.at[0], near_far),
        send(dsend.at[1 - h], drecv.at[1], pi_s.at[1], pi_r.at[1], other_far),
    ]

    for cp in first:
        cp.wait_recv()
    ring_on = hop_ring()
    cross_1 = hop_cross(1, 6) + hop_cross(3, 8)
    for cp in cross_own:
        cp.wait_recv()
    on_own = hop_cross_on(0, 10)

    for cp in pi:
        cp.wait_recv()
    dall[1 - b, k] = (drecv[0].astype(F32) + drecv[1].astype(F32)).astype(BF16)
    mine, swapped = dall.at[1 - b, k], dall.at[b, k]
    sw = send(mine, mine, sw_s, sw_r, near_far)
    f1 = send(mine, mine, f_s.at[0], f_r.at[0], flip3)

    for cp in ring_on:
        cp.wait_recv()
    cross_2 = hop_cross(2, 12)
    for cp in cross_1:
        cp.wait_recv()
    on_1 = hop_cross_on(1, 14) + hop_cross_on(3, 16)

    f1.wait_recv()
    other = dall.at[1 - b, 3 - k]
    ones = [send(mine, mine, g_s.at[0], g_r.at[0], flip1), send(other, other, g_s.at[1], g_r.at[1], flip1)]
    sw.wait_recv()
    f2 = send(swapped, swapped, f_s.at[1], f_r.at[1], flip3)
    ones.append(send(swapped, swapped, g_s.at[2], g_r.at[2], flip1))
    for cp in cross_2:
        cp.wait_recv()
    on_2 = hop_cross_on(2, 18)
    f2.wait_recv()
    other = dall.at[b, 3 - k]
    ones.append(send(other, other, g_s.at[3], g_r.at[3], flip1))
    for cp in rest:
        cp.wait()
    for cp in ones:
        cp.wait_recv()

    wide = [dall[g // 4, g % 4].astype(F32) for g in range(8)]
    docs = jnp.concatenate([w[:8] for w in wide] + [w[8:] for w in wide], axis=0).astype(BF16)
    for cp in on_own + on_1 + on_2:
        cp.wait_recv()
    nt = (((1,), (1,)), ((), ()))
    sc_b[...] = lax.dot_general(qb[...].reshape(1024, 1024), docs[:, 1024:], nt, preferred_element_type=F32).reshape(4, 4, 64, 128)
    sc_a[...] = lax.dot_general(qa[...].reshape(1024, 1024), docs[:, :1024], nt, preferred_element_type=F32).reshape(4, 4, 64, 128)

    s2 = []
    for n in range(4):
        gy = lax.rem(y + n + 1, 4)
        for gx in range(4):
            sc = sc_a[gy, gx] + sc_b[gx, gy]
            top, bottom = sc[:32], sc[32:]
            pk[0, gy, gx] = jnp.where(low, top, pltpu.roll(bottom, 64, 1))
            pk[1, gy, gx] = jnp.where(low, pltpu.roll(top, 64, 1), bottom)
        s2.append(send(pk.at[1 - c, gy], pk_recv.at[gy], s2_s.at[n], s2_r.at[n], sibling))
    os = []
    for n in range(4):
        s2[n].wait_recv()
        gy = lax.rem(y + n + 1, 4)
        fin[gy] = pk[c, gy] + pk_recv[gy]
        for dx in range(4):
            if n < 3 or dx:
                gx = lax.rem(x + dx, 4)
                os.append(send(fin.at[gy, gx], fin_recv.at[y, x], o_s.at[n * 4 + dx], o_r.at[n * 4 + dx], plane(n + 1, dx)))
    fin_recv[y, x] = fin[y, x]
    for cp in os:
        cp.wait_recv()
    for n in range(8):
        first, second = fin_recv[n // 2, 2 * (n % 2)], fin_recv[n // 2, 2 * (n % 2) + 1]
        out_ref[:32, n * 128:(n + 1) * 128] = jnp.where(low, first, pltpu.roll(second, 64, 1))
        out_ref[32:, n * 128:(n + 1) * 128] = jnp.where(low, pltpu.roll(first, 64, 1), second)

    for cp in [sib, *pi, *started, sw, f1, f2, *ones, *s2, *os]:
        cp.wait_send()


def body(proj_rows, query_features, doc_lengths, owner_map):
    vmem = pl.BlockSpec(memory_space=pltpu.VMEM)
    dma = pltpu.SemaphoreType.DMA
    return pl.pallas_call(
        kernel,
        name="scores",
        out_shape=jax.ShapeDtypeStruct((64, 1024), F32),
        in_specs=[pl.BlockSpec(memory_space=pl.ANY)] * 4,
        out_specs=vmem,
        scratch_shapes=[
            pltpu.VMEM((2048, 128), BF16),
            pltpu.VMEM((1, 32), jnp.int32),
            pltpu.VMEM((1, 32), jnp.int32),
            pltpu.VMEM((2048, 128), BF16),
            pltpu.VMEM((64, 2048), F32),
            pltpu.VMEM((32, 2048), F32),
            pltpu.VMEM((2, 32, 2048), F32),
            pltpu.VMEM((32, 2048), F32),
            pltpu.VMEM((2, 16, 2048), BF16),
            pltpu.VMEM((2, 16, 2048), BF16),
            pltpu.VMEM((2, 4, 16, 2048), BF16),
            pltpu.VMEM((4, 4, 64, 1024), BF16),
            pltpu.VMEM((4, 4, 64, 1024), BF16),
            pltpu.VMEM((4, 4, 64, 128), F32),
            pltpu.VMEM((4, 4, 64, 128), F32),
            pltpu.VMEM((2, 4, 4, 32, 128), F32),
            pltpu.VMEM((4, 4, 32, 128), F32),
            pltpu.VMEM((4, 4, 32, 128), F32),
            pltpu.VMEM((4, 4, 32, 128), F32),
            dma((3,)), dma((2,)), dma, dma, dma((2, 20)), dma((2, 20)),
            dma((2,)), dma((2,)), dma, dma, dma((2,)), dma((2,)), dma((4,)), dma((4,)),
            dma((4,)), dma((4,)), dma((16,)), dma((16,)),
        ],
        compiler_params=pltpu.CompilerParams(
            collective_id=0, has_side_effects=True, vmem_limit_bytes=48 << 20
        ),
    )(proj_rows, doc_lengths, owner_map, query_features)


def solution(mesh):
    placed = (P(("ex", "tok"), None), P("ex", None), P("ex", None), P("ex", None))
    return jax.shard_map(
        body, mesh=mesh, in_specs=placed, out_specs=P("ex", "tok"), check_vma=False
    )
```

```python
import jax
import jax.numpy as jnp
from jax import lax
from jax.experimental import pallas as pl
from jax.experimental.pallas import tpu as pltpu
from jax.sharding import PartitionSpec as P

MESH = pl.DeviceIdType.MESH
F32 = jnp.float32
BF16 = jnp.bfloat16


def kernel(
    rows_hbm, lens_hbm, owner_hbm, q_hbm, out_ref,
    rows_ref, lens_ref, owner_ref,
    gt, mask, part, sib_recv, dsend, drecv, dall, qa, qb, sc_a, sc_b, pk, pk_recv, fin, fin_recv,
    in_l, ql, sib_s, sib_r, qs, qr, pi_s, pi_r, sw_s, sw_r, f_s, f_r, g_s, g_r, s2_s, s2_r, o_s, o_r,
):
    ex, tok = lax.axis_index("ex"), lax.axis_index("tok")
    y, x, p = ex // 32, lax.rem(ex // 8, 4), lax.rem(ex, 8)
    h, c = tok // 2, lax.rem(tok, 2)
    b, k = p // 4, lax.rem(p, 4)

    def at(yy, xx_, pp, hh, cc):
        return {"ex": (yy * 4 + xx_) * 8 + pp, "tok": hh * 2 + cc}

    def plane(dy, dx):
        return at(lax.rem(y + dy, 4), lax.rem(x + dx, 4), p, h, c)

    loads = [
        pltpu.make_async_copy(src, dst, in_l.at[n])
        for n, (src, dst) in enumerate(((lens_hbm, lens_ref), (owner_hbm, owner_ref), (rows_hbm, rows_ref)))
    ]
    for cp in loads:
        cp.start()

    far = lax.rem(p + 4, 8)
    sibling = at(y, x, p, h, 1 - c)
    near_far = at(y, x, far, h, c)
    other_far = at(y, x, far, 1 - h, c)

    flip3 = at(y, x, b * 4 + 3 - k, h, c)
    flip1 = at(y, x, p + 1 - 2 * lax.rem(p, 2), h, c)

    offsets = [(dy, dx) for dy in range(4) for dx in range(4) if dy or dx]
    partners = [plane(0, 1), plane(0, 3), plane(1, 0), plane(3, 0)] + [flip3, flip1, sibling, near_far, other_far]

    barrier = pltpu.get_barrier_semaphore()
    for partner in partners:
        pl.semaphore_signal(barrier, inc=1, device_id=partner, device_id_type=MESH)

    loads[0].wait()
    loads[1].wait()
    lens = lens_ref[...].astype(F32)
    owner = owner_ref[...]
    lane = lax.broadcasted_iota(jnp.int32, (32, 32), 1)
    slot = lax.broadcasted_iota(jnp.int32, (32, 32), 0)
    match = jnp.broadcast_to(owner, (32, 32)) == slot
    lens_b = jnp.broadcast_to(lens, (32, 32))
    order = jnp.sum(jnp.where(match, lane.astype(F32), 0.0), axis=1, keepdims=True)
    size = jnp.sum(jnp.where(match, lens_b, 0.0), axis=1, keepdims=True)
    begin = jnp.sum(jnp.where(lane.astype(F32) < order, lens_b, 0.0), axis=1, keepdims=True)
    end = begin + size
    scale = 1.0 / jnp.sqrt(size)
    pos = (lax.broadcasted_iota(jnp.int32, (32, 2048), 1) + tok * 2048).astype(F32)
    mask[...] = jnp.where((pos >= begin) & (pos < end), 1.0, 0.0).astype(BF16)

    loads[2].wait()
    pick_r = lax.broadcasted_iota(jnp.int32, (64, 128), 0)
    pick_c = lax.broadcasted_iota(jnp.int32, (64, 128), 1)
    pick_g = (pick_c == pick_r + 64).astype(BF16)
    gt[...] = lax.dot_general(pick_g, rows_ref[...], (((1,), (1,)), ((), ())), preferred_element_type=F32)

    low = lax.broadcasted_iota(jnp.int32, (32, 128), 1) < 64

    def kron_half(half, dest):
        for n in range(2):
            blocks = []
            for i in range(16):
                g_row = jnp.broadcast_to(gt[pl.ds(half * 32 + n * 16 + i, 1), :], (16, 2048)).astype(BF16)
                blocks += [mask[:16] * g_row, mask[16:] * g_row]
            spread = jnp.concatenate(blocks, axis=0)
            res = jnp.dot(spread, rows_ref[...], preferred_element_type=F32)
            for i in range(8):
                even = res[64 * i:64 * i + 32]
                odd = pltpu.roll(res[64 * i + 32:64 * i + 64], 64, 1)
                dest[n, :, i * 128:(i + 1) * 128] = jnp.where(low, even, odd)

    kron_half(1 - c, part.at[0])
    kron_half(c, part.at[1])
    pl.semaphore_wait(barrier, len(partners))

    def send(src, dst, ss, rs, to):
        cp = pltpu.make_async_remote_copy(
            src_ref=src, dst_ref=dst, send_sem=ss, recv_sem=rs, device_id=to, device_id_type=MESH
        )
        cp.start()
        return cp

    sib = [send(part.at[0, n], sib_recv.at[n], sib_s.at[n], sib_r.at[n], sibling) for n in range(2)]

    halves = ((qa, y, x, lambda d: plane(0, d), lambda d: plane(d, 0)), (qb, x, y, lambda d: plane(d, 0), lambda d: plane(0, d)))
    steps = (1, 3)

    started = []

    def q_send(n, src, dst, sem, to):
        cp = send(src, dst, qs.at[n, sem], qr.at[n, sem], to)
        started.append(cp)
        return cp

    parts = (pl.ds(0, 32), pl.ds(32, 32))
    first, rest = [], []
    for n, (buf, r, s, ring, cross) in enumerate(halves):
        cols = pl.ds(pl.multiple_of(c * 2048 + n * 1024, 1024), 1024)
        own = pltpu.make_async_copy(q_hbm.at[:, cols], buf.at[r, s], ql.at[n])
        own.start()
        rest.append(own)
        for i, d in enumerate(steps):
            first.append(q_send(n, q_hbm.at[:, cols], buf.at[r, s], i, ring(d)))
    cross_own = []
    for n, (buf, r, s, ring, cross) in enumerate(halves):
        cols = pl.ds(pl.multiple_of(c * 2048 + n * 1024, 1024), 1024)
        for i, d in enumerate(steps):
            cross_own.append(q_send(n, q_hbm.at[:, cols], buf.at[r, s], 2 + i, cross(d)))

    def hop_ring():
        out = []
        for n, (buf, r, s, ring, cross) in enumerate(halves):
            for i, d in enumerate(steps):
                blk = buf.at[r, lax.rem(s + 4 - d, 4), parts[i]]
                out.append(q_send(n, blk, blk, 4 + i, ring(d)))
        return out

    def hop_cross(e, base):
        out = []
        for n, (buf, r, s, ring, cross) in enumerate(halves):
            blk = buf.at[r, lax.rem(s + e, 4)]
            for i, d in enumerate(steps):
                out.append(q_send(n, blk, blk, base + i, cross(d)))
        return out

    def hop_cross_on(e, base):
        out = []
        for n, (buf, r, s, ring, cross) in enumerate(halves):
            for i, d in enumerate(steps):
                blk = buf.at[lax.rem(r + 4 - d, 4), lax.rem(s + e, 4), parts[i]]
                out.append(q_send(n, blk, blk, base + i, cross(d)))
        return out

    pi = []
    for n in range(2):
        sib[n].wait_recv()
        feats = ((part[1, n] + sib_recv[n]) * scale).astype(BF16)
        dsend[n, 0] = feats[:16]
        dsend[n, 1] = feats[16:]
        pi.append([
            send(dsend.at[n, h], drecv.at[n, 0], pi_s.at[n, 0], pi_r.at[n, 0], near_far),
            send(dsend.at[n, 1 - h], drecv.at[n, 1], pi_s.at[n, 1], pi_r.at[n, 1], other_far),
        ])

    swaps, threes, ones = [], [], []

    def meet(n):
        for cp in pi[n]:
            cp.wait_recv()
        dall[n, 1 - b, k] = (drecv[n, 0].astype(F32) + drecv[n, 1].astype(F32)).astype(BF16)
        mine = dall.at[n, 1 - b, k]
        swaps.append(send(mine, mine, sw_s.at[n], sw_r.at[n], near_far))
        threes.append(send(mine, mine, f_s.at[n, 0], f_r.at[n, 0], flip3))
        ones.append(send(mine, mine, g_s.at[n, 0], g_r.at[n, 0], flip1))

    def far_one(n):
        threes[n].wait_recv()
        blk = dall.at[n, 1 - b, 3 - k]
        ones.append(send(blk, blk, g_s.at[n, 1], g_r.at[n, 1], flip1))

    def swapped(n):
        swaps[n].wait_recv()
        blk = dall.at[n, b, k]
        threes.append(send(blk, blk, f_s.at[n, 1], f_r.at[n, 1], flip3))
        ones.append(send(blk, blk, g_s.at[n, 2], g_r.at[n, 2], flip1))

    def far_two(n):
        threes[2 + n].wait_recv()
        blk = dall.at[n, b, 3 - k]
        ones.append(send(blk, blk, g_s.at[n, 3], g_r.at[n, 3], flip1))

    for cp in first:
        cp.wait_recv()
    ring_on = hop_ring()
    cross_1 = hop_cross(1, 6) + hop_cross(3, 8)
    for cp in cross_own:
        cp.wait_recv()
    on_own = hop_cross_on(0, 10)
    meet(0)
    for cp in ring_on:
        cp.wait_recv()
    cross_2 = hop_cross(2, 12)
    meet(1)
    for cp in cross_1:
        cp.wait_recv()
    on_1 = hop_cross_on(1, 14) + hop_cross_on(3, 16)
    far_one(0)
    swapped(0)
    far_one(1)
    swapped(1)
    for cp in cross_2:
        cp.wait_recv()
    on_2 = hop_cross_on(2, 18)
    far_two(0)
    far_two(1)
    for cp in rest:
        cp.wait()
    for cp in ones:
        cp.wait_recv()

    docs = []
    for n in range(2):
        wide = [dall[n, g // 4, g % 4].astype(F32) for g in range(8)]
        docs.append(jnp.concatenate([w[:8] for w in wide] + [w[8:] for w in wide], axis=0).astype(BF16))
    for cp in on_own + on_1 + on_2:
        cp.wait_recv()
    nt = (((1,), (1,)), ((), ()))
    sc_b[...] = lax.dot_general(qb[...].reshape(1024, 1024), docs[1], nt, preferred_element_type=F32).reshape(4, 4, 64, 128)
    sc_a[...] = lax.dot_general(qa[...].reshape(1024, 1024), docs[0], nt, preferred_element_type=F32).reshape(4, 4, 64, 128)

    s2 = []
    for n in range(4):
        gy = lax.rem(y + n + 1, 4)
        for gx in range(4):
            sc = sc_a[gy, gx] + sc_b[gx, gy]
            top, bottom = sc[:32], sc[32:]
            pk[0, gy, gx] = jnp.where(low, top, pltpu.roll(bottom, 64, 1))
            pk[1, gy, gx] = jnp.where(low, pltpu.roll(top, 64, 1), bottom)
        s2.append(send(pk.at[1 - c, gy], pk_recv.at[gy], s2_s.at[n], s2_r.at[n], sibling))
    os = []
    for n in range(4):
        s2[n].wait_recv()
        gy = lax.rem(y + n + 1, 4)
        fin[gy] = pk[c, gy] + pk_recv[gy]
        for dx in range(4):
            if n < 3 or dx:
                gx = lax.rem(x + dx, 4)
                os.append(send(fin.at[gy, gx], fin_recv.at[y, x], o_s.at[n * 4 + dx], o_r.at[n * 4 + dx], plane(n + 1, dx)))
    fin_recv[y, x] = fin[y, x]
    for cp in os:
        cp.wait_recv()
    for n in range(8):
        first, second = fin_recv[n // 2, 2 * (n % 2)], fin_recv[n // 2, 2 * (n % 2) + 1]
        out_ref[:32, n * 128:(n + 1) * 128] = jnp.where(low, first, pltpu.roll(second, 64, 1))
        out_ref[32:, n * 128:(n + 1) * 128] = jnp.where(low, pltpu.roll(first, 64, 1), second)

    for cp in [*sib, *pi[0], *pi[1], *started, *swaps, *threes, *ones, *s2, *os]:
        cp.wait_send()


def body(proj_rows, query_features, doc_lengths, owner_map):
    vmem = pl.BlockSpec(memory_space=pltpu.VMEM)
    dma = pltpu.SemaphoreType.DMA
    return pl.pallas_call(
        kernel,
        name="scores",
        out_shape=jax.ShapeDtypeStruct((64, 1024), F32),
        in_specs=[pl.BlockSpec(memory_space=pl.ANY)] * 4,
        out_specs=vmem,
        scratch_shapes=[
            pltpu.VMEM((2048, 128), BF16),
            pltpu.VMEM((1, 32), jnp.int32),
            pltpu.VMEM((1, 32), jnp.int32),
            pltpu.VMEM((64, 2048), F32),
            pltpu.VMEM((32, 2048), BF16),
            pltpu.VMEM((2, 2, 32, 1024), F32),
            pltpu.VMEM((2, 32, 1024), F32),
            pltpu.VMEM((2, 2, 16, 1024), BF16),
            pltpu.VMEM((2, 2, 16, 1024), BF16),
            pltpu.VMEM((2, 2, 4, 16, 1024), BF16),
            pltpu.VMEM((4, 4, 64, 1024), BF16),
            pltpu.VMEM((4, 4, 64, 1024), BF16),
            pltpu.VMEM((4, 4, 64, 128), F32),
            pltpu.VMEM((4, 4, 64, 128), F32),
            pltpu.VMEM((2, 4, 4, 32, 128), F32),
            pltpu.VMEM((4, 4, 32, 128), F32),
            pltpu.VMEM((4, 4, 32, 128), F32),
            pltpu.VMEM((4, 4, 32, 128), F32),
            dma((3,)), dma((2,)), dma((2,)), dma((2,)), dma((2, 20)), dma((2, 20)),
            dma((2, 2)), dma((2, 2)), dma((2,)), dma((2,)), dma((2, 2)), dma((2, 2)), dma((2, 4)), dma((2, 4)),
            dma((4,)), dma((4,)), dma((16,)), dma((16,)),
        ],
        compiler_params=pltpu.CompilerParams(
            collective_id=0, has_side_effects=True, vmem_limit_bytes=64 << 20
        ),
    )(proj_rows, doc_lengths, owner_map, query_features)


def solution(mesh):
    placed = (P(("ex", "tok"), None), P("ex", None), P("ex", None), P("ex", None))
    return jax.shard_map(
        body, mesh=mesh, in_specs=placed, out_specs=P("ex", "tok"), check_vma=False
    )
```

```python
import jax
import jax.numpy as jnp
from jax import lax
from jax.experimental import pallas as pl
from jax.experimental.pallas import tpu as pltpu
from jax.sharding import PartitionSpec as P

MESH = pl.DeviceIdType.MESH
F32 = jnp.float32
BF16 = jnp.bfloat16


def kernel(
    rows_hbm, lens_hbm, owner_hbm, q_hbm, out_ref,
    rows_ref, lens_ref, owner_ref,
    gt, mask, part, sib_recv, dsend, drecv, dall, qa, qb, pk, pk_recv, fin, fin_recv,
    in_l, ql, sib_s, sib_r, qs, qr, pi_s, pi_r, sw_s, sw_r, f_s, f_r, g_s, g_r, s2_s, s2_r, o_s, o_r, ready,
):
    ex, tok = lax.axis_index("ex"), lax.axis_index("tok")
    y, x, p = ex // 32, lax.rem(ex // 8, 4), lax.rem(ex, 8)
    h, c = tok // 2, lax.rem(tok, 2)
    b, k = p // 4, lax.rem(p, 4)

    def at(yy, xx_, pp, hh, cc):
        return {"ex": (yy * 4 + xx_) * 8 + pp, "tok": hh * 2 + cc}

    def plane(dy, dx):
        return at(lax.rem(y + dy, 4), lax.rem(x + dx, 4), p, h, c)

    loads = [
        pltpu.make_async_copy(src, dst, in_l.at[n])
        for n, (src, dst) in enumerate(((lens_hbm, lens_ref), (owner_hbm, owner_ref), (rows_hbm, rows_ref)))
    ]
    for cp in loads:
        cp.start()

    far = lax.rem(p + 4, 8)
    sibling = at(y, x, p, h, 1 - c)
    near_far = at(y, x, far, h, c)
    other_far = at(y, x, far, 1 - h, c)

    flip3 = at(y, x, b * 4 + 3 - k, h, c)
    flip1 = at(y, x, p + 1 - 2 * lax.rem(p, 2), h, c)

    z = h * 8 + p

    def along(d):
        zz = lax.rem(z + 16 + d, 16)
        return at(y, x, lax.rem(zz, 8), zz // 8, c)

    partners = [plane(0, 1), plane(0, 3), plane(1, 0), plane(3, 0), flip1, sibling, along(2), along(-2)]

    barrier = pltpu.get_barrier_semaphore()
    for partner in partners:
        pl.semaphore_signal(barrier, inc=1, device_id=partner, device_id_type=MESH)

    loads[0].wait()
    loads[1].wait()
    lens = lens_ref[...].astype(F32)
    owner = owner_ref[...]
    lane = lax.broadcasted_iota(jnp.int32, (32, 32), 1)
    slot = lax.broadcasted_iota(jnp.int32, (32, 32), 0)
    match = jnp.broadcast_to(owner, (32, 32)) == slot
    lens_b = jnp.broadcast_to(lens, (32, 32))
    order = jnp.sum(jnp.where(match, lane.astype(F32), 0.0), axis=1, keepdims=True)
    size = jnp.sum(jnp.where(match, lens_b, 0.0), axis=1, keepdims=True)
    begin = jnp.sum(jnp.where(lane.astype(F32) < order, lens_b, 0.0), axis=1, keepdims=True)
    end = begin + size
    scale = 1.0 / jnp.sqrt(size)
    pos = (lax.broadcasted_iota(jnp.int32, (32, 2048), 1) + tok * 2048).astype(F32)
    mask[...] = jnp.where((pos >= begin) & (pos < end), 1.0, 0.0).astype(BF16)

    loads[2].wait()
    pick_r = lax.broadcasted_iota(jnp.int32, (64, 128), 0)
    pick_c = lax.broadcasted_iota(jnp.int32, (64, 128), 1)
    pick_g = (pick_c == pick_r + 64).astype(BF16)
    gt[...] = lax.dot_general(pick_g, rows_ref[...], (((1,), (1,)), ((), ())), preferred_element_type=F32)

    low = lax.broadcasted_iota(jnp.int32, (32, 128), 1) < 64

    def kron_half(half, dest):
        for n in range(2):
            blocks = []
            for i in range(16):
                g_row = jnp.broadcast_to(gt[pl.ds(half * 32 + n * 16 + i, 1), :], (16, 2048)).astype(BF16)
                blocks += [mask[:16] * g_row, mask[16:] * g_row]
            spread = jnp.concatenate(blocks, axis=0)
            res = jnp.dot(spread, rows_ref[...], preferred_element_type=F32)
            for i in range(8):
                even = res[64 * i:64 * i + 32]
                odd = pltpu.roll(res[64 * i + 32:64 * i + 64], 64, 1)
                dest[n, :, i * 128:(i + 1) * 128] = jnp.where(low, even, odd)

    pl.semaphore_wait(barrier, len(partners))
    pl.semaphore_signal(ready.at[0], inc=1, device_id=along(2), device_id_type=MESH)
    pl.semaphore_signal(ready.at[1], inc=1, device_id=along(-2), device_id_type=MESH)

    def send(src, dst, ss, rs, to):
        cp = pltpu.make_async_remote_copy(
            src_ref=src, dst_ref=dst, send_sem=ss, recv_sem=rs, device_id=to, device_id_type=MESH
        )
        cp.start()
        return cp

    halves = ((qa, y, x, lambda d: plane(0, d), lambda d: plane(d, 0)), (qb, x, y, lambda d: plane(d, 0), lambda d: plane(0, d)))
    steps = (1, 3)

    started = []

    def q_send(n, src, dst, sem, to):
        cp = send(src, dst, qs.at[n, sem], qr.at[n, sem], to)
        started.append(cp)
        return cp

    parts = (pl.ds(0, 32), pl.ds(32, 32))
    first, rest = [], []
    for n, (buf, r, s, ring, cross) in enumerate(halves):
        cols = pl.ds(pl.multiple_of(c * 2048 + n * 1024, 1024), 1024)
        own = pltpu.make_async_copy(q_hbm.at[:, cols], buf.at[r, s], ql.at[n])
        own.start()
        rest.append(own)
        for i, d in enumerate(steps):
            first.append(q_send(n, q_hbm.at[:, cols], buf.at[r, s], i, ring(d)))
    cross_own = []
    for n, (buf, r, s, ring, cross) in enumerate(halves):
        cols = pl.ds(pl.multiple_of(c * 2048 + n * 1024, 1024), 1024)
        for i, d in enumerate(steps):
            cross_own.append(q_send(n, q_hbm.at[:, cols], buf.at[r, s], 2 + i, cross(d)))

    def hop_ring():
        out = []
        for n, (buf, r, s, ring, cross) in enumerate(halves):
            for i, d in enumerate(steps):
                blk = buf.at[r, lax.rem(s + 4 - d, 4), parts[i]]
                out.append(q_send(n, blk, blk, 4 + i, ring(d)))
        return out

    def hop_cross(e, base):
        out = []
        for n, (buf, r, s, ring, cross) in enumerate(halves):
            blk = buf.at[r, lax.rem(s + e, 4)]
            for i, d in enumerate(steps):
                out.append(q_send(n, blk, blk, base + i, cross(d)))
        return out

    def hop_cross_on(e, base):
        out = []
        for n, (buf, r, s, ring, cross) in enumerate(halves):
            for i, d in enumerate(steps):
                blk = buf.at[lax.rem(r + 4 - d, 4), lax.rem(s + e, 4), parts[i]]
                out.append(q_send(n, blk, blk, base + i, cross(d)))
        return out

    kron_half(1 - c, part.at[0])
    sib = [send(part.at[0, n], sib_recv.at[n], sib_s.at[n], sib_r.at[n], sibling) for n in range(2)]

    kron_half(c, part.at[1])
    pi = []
    for n in range(2):
        sib[n].wait_recv()
        if n == 0:
            pl.semaphore_wait(ready.at[0], 1)
            pl.semaphore_wait(ready.at[1], 1)
        feats = ((part[1, n] + sib_recv[n]) * scale).astype(BF16)
        dsend[n, 0] = feats[:16]
        dsend[n, 1] = feats[16:]
        pi.append([
            send(dsend.at[n, h], drecv.at[n, 0], pi_s.at[n, 0], pi_r.at[n, 0], near_far),
            send(dsend.at[n, 1 - h], drecv.at[n, 1], pi_s.at[n, 1], pi_r.at[n, 1], other_far),
        ])

    swaps, threes, ones = [], [], []

    def meet(n):
        for cp in pi[n]:
            cp.wait_recv()
        dall[n, 1 - b, k] = (drecv[n, 0].astype(F32) + drecv[n, 1].astype(F32)).astype(BF16)
        mine = dall.at[n, 1 - b, k]
        swaps.append(send(mine, mine, sw_s.at[n], sw_r.at[n], near_far))
        threes.append(send(mine, mine, f_s.at[n, 0], f_r.at[n, 0], flip3))
        ones.append(send(mine, mine, g_s.at[n, 0], g_r.at[n, 0], flip1))

    def far_one(n):
        threes[n].wait_recv()
        blk = dall.at[n, 1 - b, 3 - k]
        ones.append(send(blk, blk, g_s.at[n, 1], g_r.at[n, 1], flip1))

    def swapped(n):
        swaps[n].wait_recv()
        blk = dall.at[n, b, k]
        threes.append(send(blk, blk, f_s.at[n, 1], f_r.at[n, 1], flip3))
        ones.append(send(blk, blk, g_s.at[n, 2], g_r.at[n, 2], flip1))

    def far_two(n):
        threes[2 + n].wait_recv()
        blk = dall.at[n, b, 3 - k]
        ones.append(send(blk, blk, g_s.at[n, 3], g_r.at[n, 3], flip1))

    for cp in first:
        cp.wait_recv()
    ring_on = hop_ring()
    cross_1 = hop_cross(1, 6) + hop_cross(3, 8)
    for cp in cross_own:
        cp.wait_recv()
    on_own = hop_cross_on(0, 10)
    meet(0)
    for cp in ring_on:
        cp.wait_recv()
    cross_2 = hop_cross(2, 12)
    meet(1)
    for cp in cross_1:
        cp.wait_recv()
    on_1 = hop_cross_on(1, 14) + hop_cross_on(3, 16)
    far_one(0)
    swapped(0)
    far_one(1)
    swapped(1)
    for cp in cross_2:
        cp.wait_recv()
    on_2 = hop_cross_on(2, 18)
    far_two(0)
    far_two(1)
    for cp in rest:
        cp.wait()
    for cp in ones:
        cp.wait_recv()

    docs = []
    for n in range(2):
        wide = [dall[n, g // 4, g % 4].astype(F32) for g in range(8)]
        docs.append(jnp.concatenate([w[:8] for w in wide] + [w[8:] for w in wide], axis=0).astype(BF16))
    for cp in on_own + on_1 + on_2:
        cp.wait_recv()
    nt = (((1,), (1,)), ((), ()))
    s2, os = [], []
    turn = (2, 1, 3, 0)

    def multiply(n):
        gy = lax.rem(y + turn[n], 4)
        sc = lax.dot_general(qa[gy].reshape(256, 1024), docs[0], nt, preferred_element_type=F32)
        sc = sc + lax.dot_general(qb[:, gy].reshape(256, 1024), docs[1], nt, preferred_element_type=F32)
        for gx in range(4):
            top, bottom = sc[64 * gx:64 * gx + 32], sc[64 * gx + 32:64 * gx + 64]
            pk[0, n, gx] = jnp.where(low, top, pltpu.roll(bottom, 64, 1))
            pk[1, n, gx] = jnp.where(low, pltpu.roll(top, 64, 1), bottom)
        s2.append(send(pk.at[1 - c, n], pk_recv.at[n], s2_s.at[n], s2_r.at[n], sibling))

    def finish(n):
        s2[n].wait_recv()
        fin[n] = pk[c, n] + pk_recv[n]
        for dx in turn:
            if turn[n] or dx:
                gx = lax.rem(x + dx, 4)
                os.append(send(fin.at[n, gx], fin_recv.at[y, x], o_s.at[n, dx], o_r.at[n, dx], plane(turn[n], dx)))

    multiply(0)
    multiply(1)
    finish(0)
    multiply(2)
    finish(1)
    multiply(3)
    finish(2)
    finish(3)
    fin_recv[y, x] = fin[3, x]
    for cp in os:
        cp.wait_recv()
    for n in range(8):
        first, second = fin_recv[n // 2, 2 * (n % 2)], fin_recv[n // 2, 2 * (n % 2) + 1]
        out_ref[:32, n * 128:(n + 1) * 128] = jnp.where(low, first, pltpu.roll(second, 64, 1))
        out_ref[32:, n * 128:(n + 1) * 128] = jnp.where(low, pltpu.roll(first, 64, 1), second)

    for cp in [*sib, *pi[0], *pi[1], *started, *swaps, *threes, *ones, *s2, *os]:
        cp.wait_send()


def body(proj_rows, query_features, doc_lengths, owner_map):
    vmem = pl.BlockSpec(memory_space=pltpu.VMEM)
    dma = pltpu.SemaphoreType.DMA
    return pl.pallas_call(
        kernel,
        name="scores",
        out_shape=jax.ShapeDtypeStruct((64, 1024), F32),
        in_specs=[pl.BlockSpec(memory_space=pl.ANY)] * 4,
        out_specs=vmem,
        scratch_shapes=[
            pltpu.VMEM((2048, 128), BF16),
            pltpu.VMEM((1, 32), jnp.int32),
            pltpu.VMEM((1, 32), jnp.int32),
            pltpu.VMEM((64, 2048), F32),
            pltpu.VMEM((32, 2048), BF16),
            pltpu.VMEM((2, 2, 32, 1024), F32),
            pltpu.VMEM((2, 32, 1024), F32),
            pltpu.VMEM((2, 2, 16, 1024), BF16),
            pltpu.VMEM((2, 2, 16, 1024), BF16),
            pltpu.VMEM((2, 2, 4, 16, 1024), BF16),
            pltpu.VMEM((4, 4, 64, 1024), BF16),
            pltpu.VMEM((4, 4, 64, 1024), BF16),
            pltpu.VMEM((2, 4, 4, 32, 128), F32),
            pltpu.VMEM((4, 4, 32, 128), F32),
            pltpu.VMEM((4, 4, 32, 128), F32),
            pltpu.VMEM((4, 4, 32, 128), F32),
            dma((3,)), dma((2,)), dma((2,)), dma((2,)), dma((2, 20)), dma((2, 20)),
            dma((2, 2)), dma((2, 2)), dma((2,)), dma((2,)), dma((2, 2)), dma((2, 2)), dma((2, 4)), dma((2, 4)),
            dma((4,)), dma((4,)), dma((4, 4)), dma((4, 4)), pltpu.SemaphoreType.REGULAR((2,)),
        ],
        compiler_params=pltpu.CompilerParams(
            collective_id=0, has_side_effects=True, vmem_limit_bytes=64 << 20
        ),
    )(proj_rows, doc_lengths, owner_map, query_features)


def solution(mesh):
    placed = (P(("ex", "tok"), None), P("ex", None), P("ex", None), P("ex", None))
    return jax.shard_map(
        body, mesh=mesh, in_specs=placed, out_specs=P("ex", "tok"), check_vma=False
    )
```

```python
import jax
import jax.numpy as jnp
from jax import lax
from jax.experimental import pallas as pl
from jax.experimental.pallas import tpu as pltpu
from jax.sharding import PartitionSpec as P

MESH = pl.DeviceIdType.MESH
F32 = jnp.float32
BF16 = jnp.bfloat16


def kernel(
    rows_hbm, lens_hbm, owner_hbm, q_hbm, out_ref,
    rows_ref, lens_ref, owner_ref,
    gt, mask, part, sib_recv, dsend, drecv, dall, qa, qb, sc_a, pk, pk_recv, fin, fin_recv,
    in_l, ql, sib_s, sib_r, qs, qr, pi_s, pi_r, sw_s, sw_r, f_s, f_r, g_s, g_r, s2_s, s2_r, o_s, o_r, ready,
):
    ex, tok = lax.axis_index("ex"), lax.axis_index("tok")
    y, x, p = ex // 32, lax.rem(ex // 8, 4), lax.rem(ex, 8)
    h, c = tok // 2, lax.rem(tok, 2)
    b, k = p // 4, lax.rem(p, 4)

    def at(yy, xx_, pp, hh, cc):
        return {"ex": (yy * 4 + xx_) * 8 + pp, "tok": hh * 2 + cc}

    def plane(dy, dx):
        return at(lax.rem(y + dy, 4), lax.rem(x + dx, 4), p, h, c)

    loads = [
        pltpu.make_async_copy(src, dst, in_l.at[n])
        for n, (src, dst) in enumerate(((lens_hbm, lens_ref), (owner_hbm, owner_ref), (rows_hbm, rows_ref)))
    ]
    for cp in loads:
        cp.start()

    far = lax.rem(p + 4, 8)
    sibling = at(y, x, p, h, 1 - c)
    near_far = at(y, x, far, h, c)
    other_far = at(y, x, far, 1 - h, c)

    flip3 = at(y, x, b * 4 + 3 - k, h, c)
    flip1 = at(y, x, p + 1 - 2 * lax.rem(p, 2), h, c)

    z = h * 8 + p

    def along(d):
        zz = lax.rem(z + 16 + d, 16)
        return at(y, x, lax.rem(zz, 8), zz // 8, c)

    partners = [plane(0, 1), plane(0, 3), plane(1, 0), plane(3, 0), flip1, sibling, along(2), along(-2)]

    barrier = pltpu.get_barrier_semaphore()
    for partner in partners:
        pl.semaphore_signal(barrier, inc=1, device_id=partner, device_id_type=MESH)

    loads[0].wait()
    loads[1].wait()
    lens = lens_ref[...].astype(F32)
    owner = owner_ref[...]
    lane = lax.broadcasted_iota(jnp.int32, (32, 32), 1)
    slot = lax.broadcasted_iota(jnp.int32, (32, 32), 0)
    match = jnp.broadcast_to(owner, (32, 32)) == slot
    lens_b = jnp.broadcast_to(lens, (32, 32))
    order = jnp.sum(jnp.where(match, lane.astype(F32), 0.0), axis=1, keepdims=True)
    size = jnp.sum(jnp.where(match, lens_b, 0.0), axis=1, keepdims=True)
    begin = jnp.sum(jnp.where(lane.astype(F32) < order, lens_b, 0.0), axis=1, keepdims=True)
    end = begin + size
    scale = 1.0 / jnp.sqrt(size)
    pos = (lax.broadcasted_iota(jnp.int32, (32, 2048), 1) + tok * 2048).astype(F32)
    mask[...] = jnp.where((pos >= begin) & (pos < end), 1.0, 0.0).astype(BF16)

    loads[2].wait()
    pick_r = lax.broadcasted_iota(jnp.int32, (64, 128), 0)
    pick_c = lax.broadcasted_iota(jnp.int32, (64, 128), 1)
    pick_g = (pick_c == pick_r + 64).astype(BF16)
    gt[...] = lax.dot_general(pick_g, rows_ref[...], (((1,), (1,)), ((), ())), preferred_element_type=F32)

    low = lax.broadcasted_iota(jnp.int32, (32, 128), 1) < 64

    def kron_half(half, dest):
        for n in range(2):
            blocks = []
            for i in range(16):
                g_row = jnp.broadcast_to(gt[pl.ds(half * 32 + n * 16 + i, 1), :], (16, 2048)).astype(BF16)
                blocks += [mask[:16] * g_row, mask[16:] * g_row]
            spread = jnp.concatenate(blocks, axis=0)
            res = jnp.dot(spread, rows_ref[...], preferred_element_type=F32)
            for i in range(8):
                even = res[64 * i:64 * i + 32]
                odd = pltpu.roll(res[64 * i + 32:64 * i + 64], 64, 1)
                dest[n, :, i * 128:(i + 1) * 128] = jnp.where(low, even, odd)

    pl.semaphore_wait(barrier, len(partners))
    pl.semaphore_signal(ready.at[0], inc=1, device_id=along(2), device_id_type=MESH)
    pl.semaphore_signal(ready.at[1], inc=1, device_id=along(-2), device_id_type=MESH)

    def send(src, dst, ss, rs, to):
        cp = pltpu.make_async_remote_copy(
            src_ref=src, dst_ref=dst, send_sem=ss, recv_sem=rs, device_id=to, device_id_type=MESH
        )
        cp.start()
        return cp

    halves = ((qa, y, x, lambda d: plane(0, d), lambda d: plane(d, 0)), (qb, x, y, lambda d: plane(d, 0), lambda d: plane(0, d)))
    steps = (1, 3)

    started = []

    def q_send(n, src, dst, sem, to):
        cp = send(src, dst, qs.at[n, sem], qr.at[n, sem], to)
        started.append(cp)
        return cp

    parts = (pl.ds(0, 32), pl.ds(32, 32))
    first, rest = [], []
    for n, (buf, r, s, ring, cross) in enumerate(halves):
        cols = pl.ds(pl.multiple_of(c * 2048 + n * 1024, 1024), 1024)
        own = pltpu.make_async_copy(q_hbm.at[:, cols], buf.at[r, s], ql.at[n])
        own.start()
        rest.append(own)
        for i, d in enumerate(steps):
            first.append(q_send(n, q_hbm.at[:, cols], buf.at[r, s], i, ring(d)))
    cross_own = []
    for n, (buf, r, s, ring, cross) in enumerate(halves):
        cols = pl.ds(pl.multiple_of(c * 2048 + n * 1024, 1024), 1024)
        for i, d in enumerate(steps):
            cross_own.append(q_send(n, q_hbm.at[:, cols], buf.at[r, s], 2 + i, cross(d)))

    def hop_ring():
        out = []
        for n, (buf, r, s, ring, cross) in enumerate(halves):
            for i, d in enumerate(steps):
                blk = buf.at[r, lax.rem(s + 4 - d, 4), parts[i]]
                out.append(q_send(n, blk, blk, 4 + i, ring(d)))
        return out

    def hop_cross(e, base):
        out = []
        for n, (buf, r, s, ring, cross) in enumerate(halves):
            blk = buf.at[r, lax.rem(s + e, 4)]
            for i, d in enumerate(steps):
                out.append(q_send(n, blk, blk, base + i, cross(d)))
        return out

    def hop_cross_on(e, base):
        out = []
        for n, (buf, r, s, ring, cross) in enumerate(halves):
            for i, d in enumerate(steps):
                blk = buf.at[lax.rem(r + 4 - d, 4), lax.rem(s + e, 4), parts[i]]
                out.append(q_send(n, blk, blk, base + i, cross(d)))
        return out

    kron_half(1 - c, part.at[0])
    sib = [send(part.at[0, n], sib_recv.at[n], sib_s.at[n], sib_r.at[n], sibling) for n in range(2)]

    kron_half(c, part.at[1])
    pi = []
    for n in range(2):
        sib[n].wait_recv()
        if n == 0:
            pl.semaphore_wait(ready.at[0], 1)
            pl.semaphore_wait(ready.at[1], 1)
        feats = ((part[1, n] + sib_recv[n]) * scale).astype(BF16)
        dsend[n, 0] = feats[:16]
        dsend[n, 1] = feats[16:]
        pi.append([
            send(dsend.at[n, h], drecv.at[n, 0], pi_s.at[n, 0], pi_r.at[n, 0], near_far),
            send(dsend.at[n, 1 - h], drecv.at[n, 1], pi_s.at[n, 1], pi_r.at[n, 1], other_far),
        ])

    swaps, threes, ones, late = [], [], [], []

    def meet(n):
        for cp in pi[n]:
            cp.wait_recv()
        dall[n, 1 - b, k] = (drecv[n, 0].astype(F32) + drecv[n, 1].astype(F32)).astype(BF16)
        mine = dall.at[n, 1 - b, k]
        swaps.append(send(mine, mine, sw_s.at[n], sw_r.at[n], near_far))
        threes.append(send(mine, mine, f_s.at[n, 0], f_r.at[n, 0], flip3))
        (late if n else ones).append(send(mine, mine, g_s.at[n, 0], g_r.at[n, 0], flip1))

    def far_one(n):
        threes[n].wait_recv()
        blk = dall.at[n, 1 - b, 3 - k]
        (late if n else ones).append(send(blk, blk, g_s.at[n, 1], g_r.at[n, 1], flip1))

    def swapped(n):
        swaps[n].wait_recv()
        blk = dall.at[n, b, k]
        threes.append(send(blk, blk, f_s.at[n, 1], f_r.at[n, 1], flip3))
        (late if n else ones).append(send(blk, blk, g_s.at[n, 2], g_r.at[n, 2], flip1))

    def far_two(n):
        threes[2 + n].wait_recv()
        blk = dall.at[n, b, 3 - k]
        (late if n else ones).append(send(blk, blk, g_s.at[n, 3], g_r.at[n, 3], flip1))

    for cp in first:
        cp.wait_recv()
    ring_on = hop_ring()
    cross_1 = hop_cross(1, 6) + hop_cross(3, 8)
    for cp in cross_own:
        cp.wait_recv()
    on_own = hop_cross_on(0, 10)
    meet(0)
    for cp in ring_on:
        cp.wait_recv()
    cross_2 = hop_cross(2, 12)
    meet(1)
    for cp in cross_1:
        cp.wait_recv()
    on_1 = hop_cross_on(1, 14) + hop_cross_on(3, 16)
    far_one(0)
    swapped(0)
    far_one(1)
    swapped(1)
    for cp in cross_2:
        cp.wait_recv()
    on_2 = hop_cross_on(2, 18)
    far_two(0)
    far_two(1)
    for cp in rest:
        cp.wait()

    def documents(n):
        wide = [dall[n, g // 4, g % 4].astype(F32) for g in range(8)]
        return jnp.concatenate([w[:8] for w in wide] + [w[8:] for w in wide], axis=0).T.astype(BF16)

    turn = (2, 1, 3, 0)
    nn = (((1,), (0,)), ((), ()))

    def early(n):
        sc_a[n] = lax.dot_general(qa[lax.rem(y + turn[n], 4)].reshape(256, 1024), docs_a, nn, preferred_element_type=F32)

    for cp in ones:
        cp.wait_recv()
    docs_a = documents(0)
    for cp in on_own + on_1:
        cp.wait_recv()
    early(1)
    early(2)
    early(3)
    for cp in on_2:
        cp.wait_recv()
    early(0)
    for cp in late:
        cp.wait_recv()
    docs_b = documents(1)
    s2, os = [], []
    def multiply(n):
        gy = lax.rem(y + turn[n], 4)
        sc = sc_a[n] + lax.dot_general(qb[:, gy].reshape(256, 1024), docs_b, nn, preferred_element_type=F32)
        for gx in range(4):
            top, bottom = sc[64 * gx:64 * gx + 32], sc[64 * gx + 32:64 * gx + 64]
            pk[0, n, gx] = jnp.where(low, top, pltpu.roll(bottom, 64, 1))
            pk[1, n, gx] = jnp.where(low, pltpu.roll(top, 64, 1), bottom)
        s2.append(send(pk.at[1 - c, n], pk_recv.at[n], s2_s.at[n], s2_r.at[n], sibling))

    def finish(n):
        s2[n].wait_recv()
        fin[n] = pk[c, n] + pk_recv[n]
        for dx in turn:
            if turn[n] or dx:
                gx = lax.rem(x + dx, 4)
                os.append(send(fin.at[n, gx], fin_recv.at[y, x], o_s.at[n, dx], o_r.at[n, dx], plane(turn[n], dx)))

    multiply(0)
    multiply(1)
    finish(0)
    multiply(2)
    finish(1)
    multiply(3)
    finish(2)
    finish(3)
    fin_recv[y, x] = fin[3, x]
    for cp in os:
        cp.wait_recv()
    for n in range(8):
        first, second = fin_recv[n // 2, 2 * (n % 2)], fin_recv[n // 2, 2 * (n % 2) + 1]
        out_ref[:32, n * 128:(n + 1) * 128] = jnp.where(low, first, pltpu.roll(second, 64, 1))
        out_ref[32:, n * 128:(n + 1) * 128] = jnp.where(low, pltpu.roll(first, 64, 1), second)

    for cp in [*sib, *pi[0], *pi[1], *started, *swaps, *threes, *ones, *late, *s2, *os]:
        cp.wait_send()


def body(proj_rows, query_features, doc_lengths, owner_map):
    vmem = pl.BlockSpec(memory_space=pltpu.VMEM)
    dma = pltpu.SemaphoreType.DMA
    return pl.pallas_call(
        kernel,
        name="scores",
        out_shape=jax.ShapeDtypeStruct((64, 1024), F32),
        in_specs=[pl.BlockSpec(memory_space=pl.ANY)] * 4,
        out_specs=vmem,
        scratch_shapes=[
            pltpu.VMEM((2048, 128), BF16),
            pltpu.VMEM((1, 32), jnp.int32),
            pltpu.VMEM((1, 32), jnp.int32),
            pltpu.VMEM((64, 2048), F32),
            pltpu.VMEM((32, 2048), BF16),
            pltpu.VMEM((2, 2, 32, 1024), F32),
            pltpu.VMEM((2, 32, 1024), F32),
            pltpu.VMEM((2, 2, 16, 1024), BF16),
            pltpu.VMEM((2, 2, 16, 1024), BF16),
            pltpu.VMEM((2, 2, 4, 16, 1024), BF16),
            pltpu.VMEM((4, 4, 64, 1024), BF16),
            pltpu.VMEM((4, 4, 64, 1024), BF16),
            pltpu.VMEM((4, 256, 128), F32),
            pltpu.VMEM((2, 4, 4, 32, 128), F32),
            pltpu.VMEM((4, 4, 32, 128), F32),
            pltpu.VMEM((4, 4, 32, 128), F32),
            pltpu.VMEM((4, 4, 32, 128), F32),
            dma((3,)), dma((2,)), dma((2,)), dma((2,)), dma((2, 20)), dma((2, 20)),
            dma((2, 2)), dma((2, 2)), dma((2,)), dma((2,)), dma((2, 2)), dma((2, 2)), dma((2, 4)), dma((2, 4)),
            dma((4,)), dma((4,)), dma((4, 4)), dma((4, 4)), pltpu.SemaphoreType.REGULAR((2,)),
        ],
        compiler_params=pltpu.CompilerParams(
            collective_id=0, has_side_effects=True, vmem_limit_bytes=64 << 20
        ),
    )(proj_rows, doc_lengths, owner_map, query_features)


def solution(mesh):
    placed = (P(("ex", "tok"), None), P("ex", None), P("ex", None), P("ex", None))
    return jax.shard_map(
        body, mesh=mesh, in_specs=placed, out_specs=P("ex", "tok"), check_vma=False
    )
```

```python
import jax
import jax.numpy as jnp
from jax import lax
from jax.experimental import pallas as pl
from jax.experimental.pallas import tpu as pltpu
from jax.sharding import PartitionSpec as P

MESH = pl.DeviceIdType.MESH
F32 = jnp.float32
BF16 = jnp.bfloat16


def kernel(
    rows_hbm, lens_hbm, owner_hbm, q_hbm, out_ref,
    rows_ref, lens_ref, owner_ref,
    gt, mask, part, sib_recv, dsend, drecv, dall, qa, qb, sc_a, pk, pk_recv, fin, fin_recv,
    in_l, ql, sib_s, sib_r, qs, qr, pi_s, pi_r, sw_s, sw_r, f_s, f_r, g_s, g_r, s2_s, s2_r, o_s, o_r, ready,
):
    ex, tok = lax.axis_index("ex"), lax.axis_index("tok")
    y, x, p = ex // 32, lax.rem(ex // 8, 4), lax.rem(ex, 8)
    h, c = tok // 2, lax.rem(tok, 2)
    b, k = p // 4, lax.rem(p, 4)

    def at(yy, xx_, pp, hh, cc):
        return {"ex": (yy * 4 + xx_) * 8 + pp, "tok": hh * 2 + cc}

    def plane(dy, dx):
        return at(lax.rem(y + dy, 4), lax.rem(x + dx, 4), p, h, c)

    loads = [
        pltpu.make_async_copy(src, dst, in_l.at[n])
        for n, (src, dst) in enumerate(((lens_hbm, lens_ref), (owner_hbm, owner_ref), (rows_hbm, rows_ref)))
    ]
    for cp in loads:
        cp.start()

    far = lax.rem(p + 4, 8)
    sibling = at(y, x, p, h, 1 - c)
    near_far = at(y, x, far, h, c)
    other_far = at(y, x, far, 1 - h, c)

    flip3 = at(y, x, b * 4 + 3 - k, h, c)
    flip1 = at(y, x, p + 1 - 2 * lax.rem(p, 2), h, c)

    z = h * 8 + p

    def along(d):
        zz = lax.rem(z + 16 + d, 16)
        return at(y, x, lax.rem(zz, 8), zz // 8, c)

    partners = [plane(0, 1), plane(0, 3), plane(1, 0), plane(3, 0), flip1, sibling, along(2), along(-2)]

    barrier = pltpu.get_barrier_semaphore()
    for partner in partners:
        pl.semaphore_signal(barrier, inc=1, device_id=partner, device_id_type=MESH)

    loads[0].wait()
    loads[1].wait()
    lens = lens_ref[...].astype(F32)
    owner = owner_ref[...]
    lane = lax.broadcasted_iota(jnp.int32, (32, 32), 1)
    slot = lax.broadcasted_iota(jnp.int32, (32, 32), 0)
    match = jnp.broadcast_to(owner, (32, 32)) == slot
    lens_b = jnp.broadcast_to(lens, (32, 32))
    order = jnp.sum(jnp.where(match, lane.astype(F32), 0.0), axis=1, keepdims=True)
    size = jnp.sum(jnp.where(match, lens_b, 0.0), axis=1, keepdims=True)
    begin = jnp.sum(jnp.where(lane.astype(F32) < order, lens_b, 0.0), axis=1, keepdims=True)
    end = begin + size
    scale = 1.0 / jnp.sqrt(size)
    pos = (lax.broadcasted_iota(jnp.int32, (32, 2048), 1) + tok * 2048).astype(F32)
    mask[...] = jnp.where((pos >= begin) & (pos < end), 1.0, 0.0).astype(BF16)

    loads[2].wait()
    pick_r = lax.broadcasted_iota(jnp.int32, (64, 128), 0)
    pick_c = lax.broadcasted_iota(jnp.int32, (64, 128), 1)
    pick_g = (pick_c == pick_r + 64).astype(BF16)
    gt[...] = lax.dot_general(pick_g, rows_ref[...], (((1,), (1,)), ((), ())), preferred_element_type=F32)

    low = lax.broadcasted_iota(jnp.int32, (32, 128), 1) < 64

    def kron_half(half, dest):
        for n in range(2):
            blocks = []
            for i in range(16):
                g_row = jnp.broadcast_to(gt[pl.ds(half * 32 + n * 16 + i, 1), :], (16, 2048)).astype(BF16)
                blocks += [mask[:16] * g_row, mask[16:] * g_row]
            spread = jnp.concatenate(blocks, axis=0)
            res = jnp.dot(spread, rows_ref[...], preferred_element_type=F32)
            for i in range(8):
                even = res[64 * i:64 * i + 32]
                odd = pltpu.roll(res[64 * i + 32:64 * i + 64], 64, 1)
                dest[n, :, i * 128:(i + 1) * 128] = jnp.where(low, even, odd)

    pl.semaphore_wait(barrier, len(partners))
    pl.semaphore_signal(ready.at[0], inc=1, device_id=along(2), device_id_type=MESH)
    pl.semaphore_signal(ready.at[1], inc=1, device_id=along(-2), device_id_type=MESH)

    def send(src, dst, ss, rs, to):
        cp = pltpu.make_async_remote_copy(
            src_ref=src, dst_ref=dst, send_sem=ss, recv_sem=rs, device_id=to, device_id_type=MESH
        )
        cp.start()
        return cp

    halves = ((qa, y, x, lambda d: plane(0, d), lambda d: plane(d, 0)), (qb, x, y, lambda d: plane(d, 0), lambda d: plane(0, d)))
    steps = (1, 3)

    started = []

    def q_send(n, src, dst, sem, to):
        cp = send(src, dst, qs.at[n, sem], qr.at[n, sem], to)
        started.append(cp)
        return cp

    parts = (pl.ds(0, 32), pl.ds(32, 32))
    first, rest = [], []
    for n, (buf, r, s, ring, cross) in enumerate(halves):
        cols = pl.ds(pl.multiple_of(c * 2048 + n * 1024, 1024), 1024)
        own = pltpu.make_async_copy(q_hbm.at[:, cols], buf.at[r, s], ql.at[n])
        own.start()
        rest.append(own)
        for i, d in enumerate(steps):
            first.append(q_send(n, q_hbm.at[:, cols], buf.at[r, s], i, ring(d)))
    cross_own = []
    for n, (buf, r, s, ring, cross) in enumerate(halves):
        cols = pl.ds(pl.multiple_of(c * 2048 + n * 1024, 1024), 1024)
        for i, d in enumerate(steps):
            cross_own.append(q_send(n, q_hbm.at[:, cols], buf.at[r, s], 2 + i, cross(d)))

    def hop_ring():
        out = []
        for n, (buf, r, s, ring, cross) in enumerate(halves):
            for i, d in enumerate(steps):
                blk = buf.at[r, lax.rem(s + 4 - d, 4), parts[i]]
                out.append(q_send(n, blk, blk, 4 + i, ring(d)))
        return out

    def hop_cross(e, base):
        out = []
        for n, (buf, r, s, ring, cross) in enumerate(halves):
            blk = buf.at[r, lax.rem(s + e, 4)]
            for i, d in enumerate(steps):
                out.append(q_send(n, blk, blk, base + i, cross(d)))
        return out

    def hop_cross_on(e, base):
        out = []
        for n, (buf, r, s, ring, cross) in enumerate(halves):
            for i, d in enumerate(steps):
                blk = buf.at[lax.rem(r + 4 - d, 4), lax.rem(s + e, 4), parts[i]]
                out.append(q_send(n, blk, blk, base + i, cross(d)))
        return out

    kron_half(1 - c, part.at[0])
    sib = [send(part.at[0, n], sib_recv.at[n], sib_s.at[n], sib_r.at[n], sibling) for n in range(2)]

    kron_half(c, part.at[1])
    pi = []
    for n in range(2):
        sib[n].wait_recv()
        if n == 0:
            pl.semaphore_wait(ready.at[0], 1)
            pl.semaphore_wait(ready.at[1], 1)
        feats = ((part[1, n] + sib_recv[n]) * scale).astype(BF16)
        dsend[n, 0] = feats[:16]
        dsend[n, 1] = feats[16:]
        pi.append([
            send(dsend.at[n, h], drecv.at[n, 0], pi_s.at[n, 0], pi_r.at[n, 0], near_far),
            send(dsend.at[n, 1 - h], drecv.at[n, 1], pi_s.at[n, 1], pi_r.at[n, 1], other_far),
        ])

    swaps, threes, ones, late = [], [], [], []

    def meet(n):
        for cp in pi[n]:
            cp.wait_recv()
        dall[n, 1 - b, k] = (drecv[n, 0].astype(F32) + drecv[n, 1].astype(F32)).astype(BF16)
        mine = dall.at[n, 1 - b, k]
        swaps.append(send(mine, mine, sw_s.at[n], sw_r.at[n], near_far))
        threes.append(send(mine, mine, f_s.at[n, 0], f_r.at[n, 0], flip3))
        (late if n else ones).append(send(mine, mine, g_s.at[n, 0], g_r.at[n, 0], flip1))

    def far_one(n):
        threes[n].wait_recv()
        blk = dall.at[n, 1 - b, 3 - k]
        (late if n else ones).append(send(blk, blk, g_s.at[n, 1], g_r.at[n, 1], flip1))

    def swapped(n):
        swaps[n].wait_recv()
        blk = dall.at[n, b, k]
        threes.append(send(blk, blk, f_s.at[n, 1], f_r.at[n, 1], flip3))
        (late if n else ones).append(send(blk, blk, g_s.at[n, 2], g_r.at[n, 2], flip1))

    def far_two(n):
        threes[2 + n].wait_recv()
        blk = dall.at[n, b, 3 - k]
        (late if n else ones).append(send(blk, blk, g_s.at[n, 3], g_r.at[n, 3], flip1))

    for cp in first:
        cp.wait_recv()
    ring_on = hop_ring()
    cross_1 = hop_cross(1, 6) + hop_cross(3, 8)
    for cp in cross_own:
        cp.wait_recv()
    on_own = hop_cross_on(0, 10)
    meet(0)
    for cp in ring_on:
        cp.wait_recv()
    cross_2 = hop_cross(2, 12)
    meet(1)
    for cp in cross_1:
        cp.wait_recv()
    on_1 = hop_cross_on(1, 14) + hop_cross_on(3, 16)
    far_one(0)
    swapped(0)
    far_one(1)
    swapped(1)
    for cp in cross_2:
        cp.wait_recv()
    on_2 = hop_cross_on(2, 18)
    far_two(0)
    far_two(1)
    for cp in rest:
        cp.wait()

    def documents(n):
        wide = [dall[n, g // 4, g % 4].astype(F32) for g in range(8)]
        return jnp.concatenate([w[:8] for w in wide] + [w[8:] for w in wide], axis=0).T.astype(BF16)

    turn = (2, 1, 3, 0)
    nn = (((1,), (0,)), ((), ()))

    def early(n):
        sc_a[n] = lax.dot_general(qa[lax.rem(y + turn[n], 4)].reshape(256, 1024), docs_a, nn, preferred_element_type=F32)

    for cp in ones:
        cp.wait_recv()
    docs_a = documents(0)
    for cp in on_own + on_1:
        cp.wait_recv()
    early(1)
    early(2)
    early(3)
    for cp in on_2:
        cp.wait_recv()
    early(0)
    for cp in late:
        cp.wait_recv()
    docs_b = documents(1)
    s2, os = [], []
    def multiply(n):
        gy = lax.rem(y + turn[n], 4)
        sc = sc_a[n] + lax.dot_general(qb[:, gy].reshape(256, 1024), docs_b, nn, preferred_element_type=F32)
        for gx in range(4):
            top, bottom = sc[64 * gx:64 * gx + 32], sc[64 * gx + 32:64 * gx + 64]
            pk[0, n, gx] = jnp.where(low, top, pltpu.roll(bottom, 64, 1))
            pk[1, n, gx] = jnp.where(low, pltpu.roll(top, 64, 1), bottom)
        s2.append(send(pk.at[1 - c, n], pk_recv.at[n], s2_s.at[n], s2_r.at[n], sibling))

    def finish(n):
        s2[n].wait_recv()
        fin[n] = (pk[c, n] + pk_recv[n]).astype(BF16)
        for dx in turn:
            if turn[n] or dx:
                gx = lax.rem(x + dx, 4)
                os.append(send(fin.at[n, gx], fin_recv.at[y, x], o_s.at[n, dx], o_r.at[n, dx], plane(turn[n], dx)))

    multiply(0)
    multiply(1)
    finish(0)
    multiply(2)
    finish(1)
    multiply(3)
    finish(2)
    finish(3)
    fin_recv[y, x] = fin[3, x]
    for cp in os:
        cp.wait_recv()
    for n in range(8):
        first, second = fin_recv[n // 2, 2 * (n % 2)].astype(F32), fin_recv[n // 2, 2 * (n % 2) + 1].astype(F32)
        out_ref[:32, n * 128:(n + 1) * 128] = jnp.where(low, first, pltpu.roll(second, 64, 1))
        out_ref[32:, n * 128:(n + 1) * 128] = jnp.where(low, pltpu.roll(first, 64, 1), second)

    for cp in [*sib, *pi[0], *pi[1], *started, *swaps, *threes, *ones, *late, *s2, *os]:
        cp.wait_send()


def body(proj_rows, query_features, doc_lengths, owner_map):
    vmem = pl.BlockSpec(memory_space=pltpu.VMEM)
    dma = pltpu.SemaphoreType.DMA
    return pl.pallas_call(
        kernel,
        name="scores",
        out_shape=jax.ShapeDtypeStruct((64, 1024), F32),
        in_specs=[pl.BlockSpec(memory_space=pl.ANY)] * 4,
        out_specs=vmem,
        scratch_shapes=[
            pltpu.VMEM((2048, 128), BF16),
            pltpu.VMEM((1, 32), jnp.int32),
            pltpu.VMEM((1, 32), jnp.int32),
            pltpu.VMEM((64, 2048), F32),
            pltpu.VMEM((32, 2048), BF16),
            pltpu.VMEM((2, 2, 32, 1024), F32),
            pltpu.VMEM((2, 32, 1024), F32),
            pltpu.VMEM((2, 2, 16, 1024), BF16),
            pltpu.VMEM((2, 2, 16, 1024), BF16),
            pltpu.VMEM((2, 2, 4, 16, 1024), BF16),
            pltpu.VMEM((4, 4, 64, 1024), BF16),
            pltpu.VMEM((4, 4, 64, 1024), BF16),
            pltpu.VMEM((4, 256, 128), F32),
            pltpu.VMEM((2, 4, 4, 32, 128), F32),
            pltpu.VMEM((4, 4, 32, 128), F32),
            pltpu.VMEM((4, 4, 32, 128), BF16),
            pltpu.VMEM((4, 4, 32, 128), BF16),
            dma((3,)), dma((2,)), dma((2,)), dma((2,)), dma((2, 20)), dma((2, 20)),
            dma((2, 2)), dma((2, 2)), dma((2,)), dma((2,)), dma((2, 2)), dma((2, 2)), dma((2, 4)), dma((2, 4)),
            dma((4,)), dma((4,)), dma((4, 4)), dma((4, 4)), pltpu.SemaphoreType.REGULAR((2,)),
        ],
        compiler_params=pltpu.CompilerParams(
            collective_id=0, has_side_effects=True, vmem_limit_bytes=64 << 20
        ),
    )(proj_rows, doc_lengths, owner_map, query_features)


def solution(mesh):
    placed = (P(("ex", "tok"), None), P("ex", None), P("ex", None), P("ex", None))
    return jax.shard_map(
        body, mesh=mesh, in_specs=placed, out_specs=P("ex", "tok"), check_vma=False
    )
```

```python
import jax
import jax.numpy as jnp
from jax import lax
from jax.experimental import pallas as pl
from jax.experimental.pallas import tpu as pltpu
from jax.sharding import PartitionSpec as P

MESH = pl.DeviceIdType.MESH
F32 = jnp.float32
BF16 = jnp.bfloat16


def kernel(
    rows_hbm, lens_hbm, owner_hbm, q_hbm, out_ref,
    rows_ref, lens_ref, owner_ref,
    gt, mask, part, sib_recv, dsend, drecv, dall, qa, qb, sc_a, pk, pk_recv, fin, fin_recv,
    in_l, ql, sib_s, sib_r, qs, qr, pi_s, pi_r, sw_s, sw_r, f_s, f_r, g_s, g_r, s2_s, s2_r, o_s, o_r, ready,
):
    ex, tok = lax.axis_index("ex"), lax.axis_index("tok")
    y, x, p = ex // 32, lax.rem(ex // 8, 4), lax.rem(ex, 8)
    h, c = tok // 2, lax.rem(tok, 2)
    b, k = p // 4, lax.rem(p, 4)

    def at(yy, xx_, pp, hh, cc):
        return {"ex": (yy * 4 + xx_) * 8 + pp, "tok": hh * 2 + cc}

    def plane(dy, dx):
        return at(lax.rem(y + dy, 4), lax.rem(x + dx, 4), p, h, c)

    loads = [
        pltpu.make_async_copy(src, dst, in_l.at[n])
        for n, (src, dst) in enumerate(((lens_hbm, lens_ref), (owner_hbm, owner_ref), (rows_hbm, rows_ref)))
    ]
    for cp in loads:
        cp.start()

    far = lax.rem(p + 4, 8)
    sibling = at(y, x, p, h, 1 - c)
    near_far = at(y, x, far, h, c)
    other_far = at(y, x, far, 1 - h, c)

    flip3 = at(y, x, b * 4 + 3 - k, h, c)
    flip1 = at(y, x, p + 1 - 2 * lax.rem(p, 2), h, c)

    z = h * 8 + p

    def along(d):
        zz = lax.rem(z + 16 + d, 16)
        return at(y, x, lax.rem(zz, 8), zz // 8, c)

    partners = [plane(0, 1), plane(0, 3), plane(1, 0), plane(3, 0), flip1, sibling, along(2), along(-2)]

    barrier = pltpu.get_barrier_semaphore()
    for partner in partners:
        pl.semaphore_signal(barrier, inc=1, device_id=partner, device_id_type=MESH)

    loads[0].wait()
    loads[1].wait()
    lens = lens_ref[...].astype(F32)
    owner = owner_ref[...]
    lane = lax.broadcasted_iota(jnp.int32, (32, 32), 1)
    slot = lax.broadcasted_iota(jnp.int32, (32, 32), 0)
    match = jnp.broadcast_to(owner, (32, 32)) == slot
    lens_b = jnp.broadcast_to(lens, (32, 32))
    order = jnp.sum(jnp.where(match, lane.astype(F32), 0.0), axis=1, keepdims=True)
    size = jnp.sum(jnp.where(match, lens_b, 0.0), axis=1, keepdims=True)
    begin = jnp.sum(jnp.where(lane.astype(F32) < order, lens_b, 0.0), axis=1, keepdims=True)
    end = begin + size
    scale = 1.0 / jnp.sqrt(size)
    pos = (lax.broadcasted_iota(jnp.int32, (32, 2048), 1) + tok * 2048).astype(F32)
    mask[...] = jnp.where((pos >= begin) & (pos < end), 1.0, 0.0).astype(BF16)

    loads[2].wait()
    pick_r = lax.broadcasted_iota(jnp.int32, (64, 128), 0)
    pick_c = lax.broadcasted_iota(jnp.int32, (64, 128), 1)
    pick_g = (pick_c == pick_r + 64).astype(BF16)
    gt[...] = lax.dot_general(pick_g, rows_ref[...], (((1,), (1,)), ((), ())), preferred_element_type=F32)

    low = lax.broadcasted_iota(jnp.int32, (32, 128), 1) < 64

    def kron_half(half, dest):
        for n in range(2):
            blocks = []
            for i in range(16):
                g_row = jnp.broadcast_to(gt[pl.ds(half * 32 + n * 16 + i, 1), :], (16, 2048)).astype(BF16)
                blocks += [mask[:16] * g_row, mask[16:] * g_row]
            spread = jnp.concatenate(blocks, axis=0)
            res = jnp.dot(spread, rows_ref[...], preferred_element_type=F32)
            for i in range(8):
                even = res[64 * i:64 * i + 32]
                odd = pltpu.roll(res[64 * i + 32:64 * i + 64], 64, 1)
                dest[n, :, i * 128:(i + 1) * 128] = jnp.where(low, even, odd)

    pl.semaphore_wait(barrier, len(partners))
    pl.semaphore_signal(ready.at[0], inc=1, device_id=along(2), device_id_type=MESH)
    pl.semaphore_signal(ready.at[1], inc=1, device_id=along(-2), device_id_type=MESH)

    def send(src, dst, ss, rs, to):
        cp = pltpu.make_async_remote_copy(
            src_ref=src, dst_ref=dst, send_sem=ss, recv_sem=rs, device_id=to, device_id_type=MESH
        )
        cp.start()
        return cp

    halves = ((qa, y, x, lambda d: plane(0, d), lambda d: plane(d, 0)), (qb, x, y, lambda d: plane(d, 0), lambda d: plane(0, d)))
    steps = (1, 3)

    started = []

    def q_send(n, src, dst, sem, to):
        cp = send(src, dst, qs.at[n, sem], qr.at[n, sem], to)
        started.append(cp)
        return cp

    parts = (pl.ds(0, 32), pl.ds(32, 32))
    first, rest = [], []
    for n, (buf, r, s, ring, cross) in enumerate(halves):
        cols = pl.ds(pl.multiple_of(c * 2048 + n * 1024, 1024), 1024)
        own = pltpu.make_async_copy(q_hbm.at[:, cols], buf.at[r, s], ql.at[n])
        own.start()
        rest.append(own)
        for i, d in enumerate(steps):
            first.append(q_send(n, q_hbm.at[:, cols], buf.at[r, s], i, ring(d)))
    cross_own = []
    for n, (buf, r, s, ring, cross) in enumerate(halves):
        cols = pl.ds(pl.multiple_of(c * 2048 + n * 1024, 1024), 1024)
        for i, d in enumerate(steps):
            cross_own.append(q_send(n, q_hbm.at[:, cols], buf.at[r, s], 2 + i, cross(d)))

    def hop_ring():
        out = []
        for n, (buf, r, s, ring, cross) in enumerate(halves):
            for i, d in enumerate(steps):
                blk = buf.at[r, lax.rem(s + 4 - d, 4), parts[i]]
                out.append(q_send(n, blk, blk, 4 + i, ring(d)))
        return out

    def hop_cross(e, base):
        out = []
        for n, (buf, r, s, ring, cross) in enumerate(halves):
            blk = buf.at[r, lax.rem(s + e, 4)]
            for i, d in enumerate(steps):
                out.append(q_send(n, blk, blk, base + i, cross(d)))
        return out

    def hop_cross_on(e, base):
        out = []
        for n, (buf, r, s, ring, cross) in enumerate(halves):
            for i, d in enumerate(steps):
                blk = buf.at[lax.rem(r + 4 - d, 4), lax.rem(s + e, 4), parts[i]]
                out.append(q_send(n, blk, blk, base + i, cross(d)))
        return out

    kron_half(1 - c, part.at[0])
    sib = [send(part.at[0, n], sib_recv.at[n], sib_s.at[n], sib_r.at[n], sibling) for n in range(2)]

    kron_half(c, part.at[1])
    pi = []
    for n in range(2):
        sib[n].wait_recv()
        if n == 0:
            pl.semaphore_wait(ready.at[0], 1)
            pl.semaphore_wait(ready.at[1], 1)
        feats = ((part[1, n] + sib_recv[n]) * scale).astype(BF16)
        dsend[n, 0] = feats[:16]
        dsend[n, 1] = feats[16:]
        pi.append([
            send(dsend.at[n, h], drecv.at[n, 0], pi_s.at[n, 0], pi_r.at[n, 0], near_far),
            send(dsend.at[n, 1 - h], drecv.at[n, 1], pi_s.at[n, 1], pi_r.at[n, 1], other_far),
        ])

    swaps, threes, ones, late = [], [], [], []

    def meet(n):
        for cp in pi[n]:
            cp.wait_recv()
        dall[n, 1 - b, k] = (drecv[n, 0].astype(F32) + drecv[n, 1].astype(F32)).astype(BF16)
        mine = dall.at[n, 1 - b, k]
        swaps.append(send(mine, mine, sw_s.at[n], sw_r.at[n], near_far))
        threes.append(send(mine, mine, f_s.at[n, 0], f_r.at[n, 0], flip3))
        (late if n else ones).append(send(mine, mine, g_s.at[n, 0], g_r.at[n, 0], flip1))

    def far_one(n):
        threes[n].wait_recv()
        blk = dall.at[n, 1 - b, 3 - k]
        (late if n else ones).append(send(blk, blk, g_s.at[n, 1], g_r.at[n, 1], flip1))

    def swapped(n):
        swaps[n].wait_recv()
        blk = dall.at[n, b, k]
        threes.append(send(blk, blk, f_s.at[n, 1], f_r.at[n, 1], flip3))
        (late if n else ones).append(send(blk, blk, g_s.at[n, 2], g_r.at[n, 2], flip1))

    def far_two(n):
        threes[2 + n].wait_recv()
        blk = dall.at[n, b, 3 - k]
        (late if n else ones).append(send(blk, blk, g_s.at[n, 3], g_r.at[n, 3], flip1))

    for cp in first:
        cp.wait_recv()
    ring_on = hop_ring()
    cross_1 = hop_cross(1, 6) + hop_cross(3, 8)
    for cp in cross_own:
        cp.wait_recv()
    on_own = hop_cross_on(0, 10)
    meet(0)
    for cp in ring_on:
        cp.wait_recv()
    cross_2 = hop_cross(2, 12)
    meet(1)
    for cp in cross_1:
        cp.wait_recv()
    on_1 = hop_cross_on(1, 14) + hop_cross_on(3, 16)
    far_one(0)
    swapped(0)
    far_one(1)
    swapped(1)
    for cp in cross_2:
        cp.wait_recv()
    on_2 = hop_cross_on(2, 18)
    far_two(0)
    far_two(1)
    for cp in rest:
        cp.wait()

    def documents(n):
        wide = [dall[n, g // 4, g % 4].astype(F32) for g in range(8)]
        return jnp.concatenate([w[:8] for w in wide] + [w[8:] for w in wide], axis=0).T.astype(BF16)

    turn = (2, 1, 3, 0)
    nn = (((1,), (0,)), ((), ()))

    def early(n):
        sc_a[n] = lax.dot_general(qa[lax.rem(y + turn[n], 4)].reshape(256, 1024), docs_a, nn, preferred_element_type=F32)

    for cp in ones:
        cp.wait_recv()
    docs_a = documents(0)
    for cp in on_own + on_1:
        cp.wait_recv()
    early(1)
    early(2)
    early(3)
    for cp in on_2:
        cp.wait_recv()
    early(0)
    for cp in late:
        cp.wait_recv()
    docs_b = documents(1)
    s2, os = [], []
    def multiply(n):
        gy = lax.rem(y + turn[n], 4)
        sc = sc_a[n] + lax.dot_general(qb[:, gy].reshape(256, 1024), docs_b, nn, preferred_element_type=F32)
        for gx in range(4):
            top, bottom = sc[64 * gx:64 * gx + 32], sc[64 * gx + 32:64 * gx + 64]
            pk[0, n, gx] = jnp.where(low, top, pltpu.roll(bottom, 64, 1))
            pk[1, n, gx] = jnp.where(low, pltpu.roll(top, 64, 1), bottom)
        s2.append(send(pk.at[1 - c, n], pk_recv.at[n], s2_s.at[n], s2_r.at[n], sibling))

    def finish(n):
        s2[n].wait_recv()
        fin[n] = (pk[c, n] + pk_recv[n]).astype(BF16)
        for dx in turn:
            if turn[n] or dx:
                gx = lax.rem(x + dx, 4)
                os.append(send(fin.at[n, gx], fin_recv.at[y, x], o_s.at[n, dx], o_r.at[n, dx], plane(turn[n], dx)))

    multiply(0)
    multiply(1)
    finish(0)
    multiply(2)
    finish(1)
    multiply(3)
    finish(2)
    finish(3)
    fin_recv[y, x] = fin[3, x]
    for n in (3, 1, 2, 0):
        for cp in os[4 * n:4 * n + 4]:
            cp.wait_recv()
        gy = lax.rem(y + 4 - turn[n], 4)
        for m in range(2):
            left, right = fin_recv[gy, 2 * m].astype(F32), fin_recv[gy, 2 * m + 1].astype(F32)
            cols = pl.ds(pl.multiple_of(gy * 256 + m * 128, 128), 128)
            out_ref[:32, cols] = jnp.where(low, left, pltpu.roll(right, 64, 1))
            out_ref[32:, cols] = jnp.where(low, pltpu.roll(left, 64, 1), right)

    for cp in [*sib, *pi[0], *pi[1], *started, *swaps, *threes, *ones, *late, *s2, *os]:
        cp.wait_send()


def body(proj_rows, query_features, doc_lengths, owner_map):
    vmem = pl.BlockSpec(memory_space=pltpu.VMEM)
    dma = pltpu.SemaphoreType.DMA
    return pl.pallas_call(
        kernel,
        name="scores",
        out_shape=jax.ShapeDtypeStruct((64, 1024), F32),
        in_specs=[pl.BlockSpec(memory_space=pl.ANY)] * 4,
        out_specs=vmem,
        scratch_shapes=[
            pltpu.VMEM((2048, 128), BF16),
            pltpu.VMEM((1, 32), jnp.int32),
            pltpu.VMEM((1, 32), jnp.int32),
            pltpu.VMEM((64, 2048), F32),
            pltpu.VMEM((32, 2048), BF16),
            pltpu.VMEM((2, 2, 32, 1024), F32),
            pltpu.VMEM((2, 32, 1024), F32),
            pltpu.VMEM((2, 2, 16, 1024), BF16),
            pltpu.VMEM((2, 2, 16, 1024), BF16),
            pltpu.VMEM((2, 2, 4, 16, 1024), BF16),
            pltpu.VMEM((4, 4, 64, 1024), BF16),
            pltpu.VMEM((4, 4, 64, 1024), BF16),
            pltpu.VMEM((4, 256, 128), F32),
            pltpu.VMEM((2, 4, 4, 32, 128), F32),
            pltpu.VMEM((4, 4, 32, 128), F32),
            pltpu.VMEM((4, 4, 32, 128), BF16),
            pltpu.VMEM((4, 4, 32, 128), BF16),
            dma((3,)), dma((2,)), dma((2,)), dma((2,)), dma((2, 20)), dma((2, 20)),
            dma((2, 2)), dma((2, 2)), dma((2,)), dma((2,)), dma((2, 2)), dma((2, 2)), dma((2, 4)), dma((2, 4)),
            dma((4,)), dma((4,)), dma((4, 4)), dma((4, 4)), pltpu.SemaphoreType.REGULAR((2,)),
        ],
        compiler_params=pltpu.CompilerParams(
            collective_id=0, has_side_effects=True, vmem_limit_bytes=64 << 20
        ),
    )(proj_rows, doc_lengths, owner_map, query_features)


def solution(mesh):
    placed = (P(("ex", "tok"), None), P("ex", None), P("ex", None), P("ex", None))
    return jax.shard_map(
        body, mesh=mesh, in_specs=placed, out_specs=P("ex", "tok"), check_vma=False
    )
```
